32 devices in a mesh: tp: 8 (over z, y), dp: 4 (over x, core).
Axes of the slice: x: 2, y: 2, z: 4, core: 2. Of those that a mesh axis runs over, the one named last changes fastest.
Arguments:
- tokens: bfloat16 [4, 16, 4096], P('dp', 'tp'), may hold values from -6 to 6
- gate_weight: bfloat16 [4096, 16384], P('dp', 'tp'), may hold values from -0.09375 to 0.09375
- up_weight: bfloat16 [4096, 16384], P('dp', 'tp'), may hold values from -0.09375 to 0.09375
- cotangent: bfloat16 [4, 16, 16384], P('dp', None, 'tp'), may hold values from -6 to 6
Outputs:
- hidden: bfloat16 [4, 16, 16384], P('dp', None, 'tp')
- grad_tokens: bfloat16 [4, 16, 4096], P('dp', 'tp')
- grad_gate: bfloat16 [4096, 16384], P(None, 'tp')
- grad_up: bfloat16 [4096, 16384], P(None, 'tp')
The draws below stay inside these ranges and needn't reach their ends.
All inputs are finite; a program needn't handle non-finite values.
Results may differ from the reference program's by a relative error of at most 0.009.
Values may be sent and summed in bfloat16 or wider, within the bound.
No kernel may reach another device: no remote copies, remote signals or barrier semaphores. Data moves between devices by JAX's collectives and lax.ppermute only.
A program may use at most 320 MiB of HBM per device.

```python
import jax
import jax.numpy as jnp
from jax import lax

D = 4096
FF = 16384
TOKENS = 16
N_DP = 4


def raised(entries, own_key, source, target, blocks, factor):
    def block_of(dim):
        return (jnp.arange(entries.shape[dim]) // (entries.shape[dim] // blocks)).reshape((-1,) + (1,) * (entries.ndim - 1 - dim))

    one_side = jax.random.permutation(own_key, blocks)[block_of(target)]
    far = (block_of(target) + blocks // 2) % blocks
    return jnp.where((block_of(source) == one_side) | (block_of(source) == far), factor * entries, entries)


def block_scale(stream_key, extent, shards, least, high):
    def one(dim, shards_of):
        steps = jax.random.uniform(jax.random.fold_in(jax.random.fold_in(stream_key, 6), dim), (shards_of,), jnp.float32, least / len(shards), high / len(shards))
        return jnp.repeat(jnp.exp(steps), extent[dim] // shards_of).reshape((-1,) + (1,) * (len(extent) - dim - 1))

    factor_of = one(*shards[0])
    for cut in shards[1:]:
        factor_of = factor_of * one(*cut)
    return factor_of


def noise(key, shape, scale, bound, split=(), held_as=jnp.bfloat16):
    result = scale * jax.random.normal(key, shape, jnp.float32)
    if split:
        result = result * block_scale(key, shape, split, -0.22, 0.18)
    return jnp.clip(result, -bound, bound).astype(held_as)


def bell_draw_with(rng, dims, width, most, pieces, heavy, kind=jnp.bfloat16):
    values = width * jax.random.normal(rng, dims, jnp.float32)
    if pieces:
        values = values * block_scale(rng, dims, pieces, -0.22, 0.18)
    return jnp.clip(raised(values, jax.random.fold_in(rng, 3), *heavy), -most, most).astype(kind)


def setup_inputs(seed: int = 0) -> dict:
    seeds = jax.random.split(jax.random.key(seed), 5)
    tokens = noise(seeds[0], (N_DP, TOKENS, D), 1.0, 6.0, ((0, 4), (1, 8)))
    gate_weight = noise(seeds[1], (D, FF), D ** -0.5, 0.09375, ((0, 4), (1, 8)))
    up_weight = noise(seeds[2], (D, FF), D ** -0.5, 0.09375, ((0, 4), (1, 8)))
    cotangent = bell_draw_with(seeds[3], (N_DP, TOKENS, FF), 1.0, 6.0, ((0, 4), (2, 8)), (2, 1, 8, 2.0))
    return dict(tokens=tokens, gate_weight=gate_weight, up_weight=up_weight, cotangent=cotangent)


def swish_parts(gate_pre):
    sigmoid_val = jax.nn.sigmoid(gate_pre)
    return gate_pre * sigmoid_val, sigmoid_val * (1.0 + gate_pre * (1.0 - sigmoid_val))


def reference(tokens, gate_weight, up_weight, cotangent):
    def per_replica(totals, inputs):
        own_rows, grad_hidden = inputs
        gate_pre = jnp.dot(own_rows, gate_weight, preferred_element_type=jnp.float32)
        up_pre = jnp.dot(own_rows, up_weight, preferred_element_type=jnp.float32)
        swish_act, swish_slope = swish_parts(gate_pre)
        hidden = (swish_act * up_pre).astype(jnp.bfloat16)
        back_float = grad_hidden.astype(jnp.float32)
        d_gate = (back_float * up_pre * swish_slope).astype(jnp.bfloat16)
        d_up = (back_float * swish_act).astype(jnp.bfloat16)
        grad_rows = jnp.dot(d_gate, gate_weight.T, preferred_element_type=jnp.float32)
        grad_rows = (grad_rows + jnp.dot(d_up, up_weight.T, preferred_element_type=jnp.float32)).astype(jnp.bfloat16)
        part_gate = lax.optimization_barrier(jnp.dot(own_rows.T, d_gate, preferred_element_type=jnp.float32).astype(jnp.bfloat16))
        part_up = lax.optimization_barrier(jnp.dot(own_rows.T, d_up, preferred_element_type=jnp.float32).astype(jnp.bfloat16))
        totals = (totals[0] + part_gate.astype(jnp.float32), totals[1] + part_up.astype(jnp.float32))
        return totals, (hidden, grad_rows)

    zero_grads = (jnp.zeros((D, FF), jnp.float32), jnp.zeros((D, FF), jnp.float32))
    (sum_gate, sum_up), (hidden, grad_tokens) = lax.scan(per_replica, zero_grads, (tokens, cotangent))
    inverse_dp = 1.0 / N_DP
    return hidden, grad_tokens, (sum_gate * inverse_dp).astype(jnp.bfloat16), (sum_up * inverse_dp).astype(jnp.bfloat16)
```

```python
import jax
import jax.numpy as jnp
from jax import lax
from jax.sharding import PartitionSpec as P

F32 = jnp.float32
BF16 = jnp.bfloat16


def swap(value, axis, bit):
    return lax.ppermute(value, axis, [(i, i ^ bit) for i in range(lax.axis_size(axis))])


def bits_of(size):
    assert size & (size - 1) == 0
    return [1 << k for k in reversed(range(size.bit_length() - 1))]


def swish_parts(gate_pre):
    s = jax.nn.sigmoid(gate_pre)
    return gate_pre * s, s * (1.0 + gate_pre * (1.0 - s))


def shards(tokens, gate_weight, up_weight, cotangent):
    n_tp, n_dp = lax.axis_size("tp"), lax.axis_size("dp")
    assert n_dp == 4
    t, r = lax.axis_index("tp"), lax.axis_index("dp")
    _, rt, d_model = tokens.shape
    depth, width = gate_weight.shape
    rows = rt * n_tp
    rel = [0]
    for bit in bits_of(n_tp):
        rel = rel + [v ^ bit for v in rel]
    rel = jnp.array(rel)

    own = tokens[0].reshape(rt, n_dp, depth)
    own = jnp.take(own, r ^ jnp.arange(n_dp), axis=1).transpose(1, 0, 2).reshape(2, 2, rt, depth)
    part = jnp.stack([own[0], swap(own[1], "dp", 2)], axis=1)
    part = jnp.stack([part[0], swap(part[1], "dp", 1)])
    part = part[:, :, None]
    for bit in bits_of(n_tp):
        part = jnp.concatenate([part, swap(part, "tp", bit)], axis=2)
    feats = part.reshape(4 * rows, depth)

    cot = cotangent[0].reshape(n_tp, rt, width)
    cot = jnp.take(cot, t ^ rel, axis=0).reshape(rows, width)
    cot = jnp.concatenate([cot, swap(cot, "dp", 2)])

    def across(v):
        return v.reshape((-1, 2) + v.shape[1:])[:, ::-1].reshape(v.shape)

    def pre(weight):
        out = jnp.dot(feats, weight, preferred_element_type=F32)
        half = (out[: 2 * rows] + swap(out[2 * rows :], "dp", 1)).astype(BF16)
        other = swap(half, "dp", 2)
        other = jnp.concatenate([other[rows:], other[:rows]])
        return half.astype(F32) + other.astype(F32)

    gate_pre, up_pre = pre(gate_weight), pre(up_weight)
    act, slope = swish_parts(gate_pre)
    hidden = (act * up_pre)[:rows].astype(BF16).reshape(n_tp, rt, width)
    place = jnp.argsort(rel)
    hidden = jnp.take(hidden, place[t ^ jnp.arange(n_tp)], axis=0).reshape(1, rows, width)
    back = cot.astype(F32)
    d_gate = (back * up_pre * slope).astype(BF16)
    d_up = (back * act).astype(BF16)
    d_gate = jnp.concatenate([d_gate, swap(d_gate, "dp", 1)])
    d_up = jnp.concatenate([d_up, swap(d_up, "dp", 1)])

    feats4 = feats.reshape(2, 2, rows, depth)
    feats4 = jnp.stack([feats4, swap(feats4, "dp", 2)[:, ::-1]])
    feats4 = jnp.stack([feats4, swap(feats4, "dp", 1)[:, ::-1]])
    feats4 = feats4.transpose(1, 0, 2, 3, 4, 5).reshape(n_dp, 4 * rows, depth)
    whole = jnp.take(feats4, r ^ jnp.arange(n_dp), axis=0).transpose(1, 0, 2).reshape(4 * rows, d_model)

    cols = (((1,), (1,)), ((), ()))
    total = lax.dot_general(d_gate, gate_weight, cols, preferred_element_type=F32)
    total = total + lax.dot_general(d_up, up_weight, cols, preferred_element_type=F32)
    total = total.reshape(2, 2, n_tp, rt, depth)
    for bit in reversed(bits_of(n_tp)):
        mid = total.shape[2] // 2
        total = total[:, :, :mid] + swap(total[:, :, mid:], "tp", bit)
    total = total[:, :, 0]
    total = jnp.stack([total[:, 0], swap(total[:, 1], "dp", 2)], axis=1)
    total = jnp.stack([total[0], swap(total[1], "dp", 1)])
    total = total.transpose(1, 0, 2, 3).reshape(n_dp, rt, depth)
    total = jnp.take(total, r ^ jnp.arange(n_dp), axis=0).transpose(1, 0, 2)
    grad_tokens = total.reshape(1, rt, d_model).astype(BF16)

    down = (((0,), (0,)), ((), ()))
    inverse = 1.0 / n_dp
    grad_gate = (lax.dot_general(whole, d_gate, down, preferred_element_type=F32) * inverse).astype(BF16)
    grad_up = (lax.dot_general(whole, d_up, down, preferred_element_type=F32) * inverse).astype(BF16)
    return hidden, grad_tokens, grad_gate, grad_up


def solution(mesh):
    in_specs = (P("dp", "tp", None), P("dp", "tp"), P("dp", "tp"), P("dp", None, "tp"))
    out_specs = (P("dp", None, "tp"), P("dp", "tp", None), P(None, "tp"), P(None, "tp"))
    return jax.shard_map(shards, mesh=mesh, in_specs=in_specs, out_specs=out_specs, check_vma=False)
```

```python
import functools

import jax
import jax.numpy as jnp
from jax import lax
from jax.experimental import pallas as pl
from jax.experimental.pallas import tpu as pltpu
from jax.sharding import PartitionSpec as P


F32 = jnp.float32
BF16 = jnp.bfloat16
VMEM = pl.BlockSpec(memory_space=pltpu.VMEM)
ANY = pl.BlockSpec(memory_space=pl.ANY)


def swap(value, tp_mask, dp_mask):
    n_tp, n_dp = lax.axis_size("tp"), lax.axis_size("dp")
    pairs = [(t * n_dp + r, (t ^ tp_mask) * n_dp + (r ^ dp_mask)) for t in range(n_tp) for r in range(n_dp)]
    return lax.ppermute(value, ("tp", "dp"), pairs)


def bits_of(size):
    assert size & (size - 1) == 0
    return [1 << k for k in reversed(range(size.bit_length() - 1))]


def swish_parts(gate_pre):
    s = jax.nn.sigmoid(gate_pre)
    return gate_pre * s, s * (1.0 + gate_pre * (1.0 - s))


def load_kernel(w_ref, o_ref, sem):
    copy = pltpu.make_async_copy(w_ref, o_ref, sem)
    copy.start()
    copy.wait()


def load(weight):
    return pl.pallas_call(
        load_kernel,
        in_specs=[ANY],
        out_specs=VMEM,
        out_shape=pltpu.VMEM(weight.shape, weight.dtype),
        scratch_shapes=[pltpu.SemaphoreType.DMA],
        compiler_params=pltpu.CompilerParams(vmem_limit_bytes=1 << 20),
        cost_estimate=pl.CostEstimate(flops=0, bytes_accessed=2 * weight.size, transcendentals=0),
    )(weight)


def outer_kernel(rows_ref, grad_ref, *rest, base, steps, scale):
    out_ref, buf, sem = rest[-3:]
    slots, tall, wide = buf.shape
    across = grad_ref.shape[1] // wide
    depth = slots // across

    def copy(step, col):
        slot = lax.rem(step, depth) * across + col
        top = pl.multiple_of((base + step) * tall, tall)
        return pltpu.make_async_copy(
            buf.at[slot], out_ref.at[pl.ds(top, tall), pl.ds(col * wide, wide)], sem.at[slot]
        )

    def body(step, carry):
        top = pl.multiple_of((base + step) * tall, tall)
        left = rows_ref[:, pl.ds(top, tall)]
        for col in range(across):

            @pl.when(step >= depth)
            def _():
                copy(step - depth, col).wait()

            acc = lax.dot_general(
                left, grad_ref[:, col * wide : (col + 1) * wide], (((0,), (0,)), ((), ())), preferred_element_type=F32
            )
            buf[lax.rem(step, depth) * across + col] = (acc * scale).astype(BF16)
            copy(step, col).start()
        return carry

    lax.fori_loop(0, steps, body, 0)
    for step in range(max(0, steps - depth), steps):
        for col in range(across):
            copy(step, col).wait()


def outer(rows, grad, scale, begin, share, whole=None):
    count, d_model = rows.shape
    width = grad.shape[1]
    tall, wide = min(512, d_model // share), min(1024, width)
    steps = d_model // share // tall
    slots = 2 * (width // wide)
    kernel = functools.partial(outer_kernel, base=begin * steps, steps=steps, scale=scale)
    args = (rows, grad) if whole is None else (rows, grad, whole)
    return pl.pallas_call(
        kernel,
        in_specs=[VMEM, VMEM] + [ANY] * (len(args) - 2),
        out_specs=ANY,
        out_shape=jax.ShapeDtypeStruct((d_model, width), BF16),
        input_output_aliases={2: 0} if whole is not None else {},
        scratch_shapes=[pltpu.VMEM((slots, tall, wide), BF16), pltpu.SemaphoreType.DMA((slots,))],
        compiler_params=pltpu.CompilerParams(vmem_limit_bytes=24 << 20),
        cost_estimate=pl.CostEstimate(
            flops=2 * count * d_model * width // share,
            bytes_accessed=2 * d_model * width // share + 2 * count * (d_model + width),
            transcendentals=0,
        ),
    )(*args)


def shards(tokens, gate_weight, up_weight, cotangent):
    n_tp, n_dp = lax.axis_size("tp"), lax.axis_size("dp")
    assert n_dp == 4
    t, r = lax.axis_index("tp"), lax.axis_index("dp")
    _, rt, d_model = tokens.shape
    depth, width = gate_weight.shape
    rows = rt * n_tp
    rel = [0]
    for bit in bits_of(n_tp):
        rel = rel + [v ^ bit for v in rel]
    odd = jnp.array([v.bit_count() % 2 == 1 for v in rel])[None, :, None, None]
    place = [rel.index(v) for v in range(n_tp)]
    rel, place = jnp.array(rel), jnp.array(place)

    cot = swap(cotangent[0], 0, 3)
    cot = jnp.stack([cotangent[0], cot]).reshape(2, n_tp, rt, width)
    cot = jnp.take(cot, t ^ rel, axis=1).reshape(2 * rows, width)

    part = tokens
    for bit in bits_of(n_tp):
        part = jnp.concatenate([part, swap(part, bit, 1)])
    part = jnp.stack([part, swap(part, 0, 3)])
    far = swap(part, 0, 1)
    feats = jnp.stack([jnp.where(odd, far, part), jnp.where(odd, part, far)])
    feats = feats.reshape(4 * rows, d_model)
    own = lax.dynamic_slice(feats, (0, r * depth), (4 * rows, depth))
    gate_weight = load(gate_weight)
    up_weight = load(up_weight)

    def pre(weight):
        out = jnp.dot(own, weight, preferred_element_type=F32)
        half = (out[: 2 * rows] + swap(out[2 * rows :], 0, 1)).astype(BF16)
        other = swap(half, 0, 3)
        other = jnp.concatenate([other[rows:], other[:rows]])
        return half.astype(F32) + other.astype(F32)

    gate_pre, up_pre = pre(gate_weight), pre(up_weight)
    act, slope = swish_parts(gate_pre)
    hidden = (act * up_pre)[:rows].astype(BF16).reshape(n_tp, rt, width)
    hidden = jnp.take(hidden, place[t ^ jnp.arange(n_tp)], axis=0).reshape(1, rows, width)
    back = cot.astype(F32)
    d_gate = (back * up_pre * slope).astype(BF16)
    d_up = (back * act).astype(BF16)
    d_gate = jnp.concatenate([d_gate, swap(d_gate, 0, 1)])
    d_up = jnp.concatenate([d_up, swap(d_up, 0, 1)])

    cols = (((1,), (1,)), ((), ()))
    total = lax.dot_general(d_gate, gate_weight, cols, preferred_element_type=F32)
    total = total + lax.dot_general(d_up, up_weight, cols, preferred_element_type=F32)
    total = total.reshape(2, 2, n_tp, rt, depth)
    for bit in reversed(bits_of(n_tp)):
        mid = total.shape[2] // 2
        total = total[:, :, :mid] + swap(total[:, :, mid:], bit, 0)
    total = total[:, :, 0]
    total = jnp.stack([total[:, 0], swap(total[:, 1], 0, 3)], axis=1)
    total = jnp.stack([total[0], swap(total[1], 0, 1)])
    total = total.reshape(n_dp, rt, depth)
    at = jnp.array([0, 2, 3, 1])
    total = jnp.take(total, at[r ^ jnp.arange(n_dp)], axis=0).transpose(1, 0, 2)
    grad_tokens = total.reshape(1, rt, d_model).astype(BF16)

    inverse = 1.0 / n_dp
    grad_gate = outer(feats, d_gate, inverse, 0, 2)
    grad_gate = outer(feats, d_gate, inverse, 1, 2, grad_gate)
    grad_up = outer(feats, d_up, inverse, 0, 2)
    grad_up = outer(feats, d_up, inverse, 1, 2, grad_up)
    return hidden, grad_tokens, grad_gate, grad_up


def solution(mesh):
    in_specs = (P("dp", "tp", None), P("dp", "tp"), P("dp", "tp"), P("dp", None, "tp"))
    out_specs = (P("dp", None, "tp"), P("dp", "tp", None), P(None, "tp"), P(None, "tp"))

    return jax.shard_map(shards, mesh=mesh, in_specs=in_specs, out_specs=out_specs, check_vma=False)
```

```python
import functools

import jax
import jax.numpy as jnp
from jax import lax
from jax.experimental import pallas as pl
from jax.experimental.pallas import tpu as pltpu
from jax.sharding import PartitionSpec as P


F32 = jnp.float32
BF16 = jnp.bfloat16
VMEM = pl.BlockSpec(memory_space=pltpu.VMEM)
HBM = pl.BlockSpec(memory_space=pltpu.HBM)


def swap(value, tp_mask, dp_mask):
    n_tp, n_dp = lax.axis_size("tp"), lax.axis_size("dp")
    pairs = [(t * n_dp + r, (t ^ tp_mask) * n_dp + (r ^ dp_mask)) for t in range(n_tp) for r in range(n_dp)]
    return lax.ppermute(value, ("tp", "dp"), pairs)


def bits_of(size):
    assert size & (size - 1) == 0
    return [1 << k for k in reversed(range(size.bit_length() - 1))]


def swish_parts(gate_pre):
    s = jax.nn.sigmoid(gate_pre)
    return gate_pre * s, s * (1.0 + gate_pre * (1.0 - s))


def outer_kernel(rows_ref, grad_ref, *rest, base, steps, scale):
    out_ref, buf, sem = rest[-3:]
    depth, tall, width = buf.shape
    wide = min(512, width)

    def copy(step):
        top = pl.multiple_of((base + step) * tall, tall)
        slot = lax.rem(step, depth)
        return pltpu.make_async_copy(buf.at[slot], out_ref.at[pl.ds(top, tall), :], sem.at[slot])

    def body(step, carry):
        top = pl.multiple_of((base + step) * tall, tall)
        left = rows_ref[:, pl.ds(top, tall)]

        @pl.when(step >= depth)
        def _():
            copy(step - depth).wait()

        for at in range(0, width, wide):
            acc = lax.dot_general(
                left, grad_ref[:, at : at + wide], (((0,), (0,)), ((), ())), preferred_element_type=F32
            )
            buf[lax.rem(step, depth), :, at : at + wide] = (acc * scale).astype(BF16)
        copy(step).start()
        return carry

    lax.fori_loop(0, steps, body, 0)
    for step in range(max(0, steps - depth), steps):
        copy(step).wait()


def outer(rows, grad, scale, begin, share, whole=None):
    count, d_model = rows.shape
    width = grad.shape[1]
    tall = min(1024, d_model // share)
    steps = d_model // share // tall
    kernel = functools.partial(outer_kernel, base=begin * steps, steps=steps, scale=scale)
    args = (rows, grad) if whole is None else (rows, grad, whole)
    return pl.pallas_call(
        kernel,
        in_specs=[VMEM, VMEM] + [HBM] * (len(args) - 2),
        out_specs=HBM,
        out_shape=jax.ShapeDtypeStruct((d_model, width), BF16),
        input_output_aliases={2: 0} if whole is not None else {},
        scratch_shapes=[pltpu.VMEM((2, tall, width), BF16), pltpu.SemaphoreType.DMA((2,))],
        compiler_params=pltpu.CompilerParams(vmem_limit_bytes=20 << 20),
        cost_estimate=pl.CostEstimate(
            flops=2 * count * d_model * width // share,
            bytes_accessed=2 * d_model * width // share + 2 * count * (d_model + width),
            transcendentals=0,
        ),
    )(*args)


def shards(tokens, gate_weight, up_weight, cotangent):
    n_tp, n_dp = lax.axis_size("tp"), lax.axis_size("dp")
    assert n_dp == 4
    t, r = lax.axis_index("tp"), lax.axis_index("dp")
    _, rt, d_model = tokens.shape
    depth, width = gate_weight.shape
    rows = rt * n_tp
    rel = [0]
    for bit in bits_of(n_tp):
        rel = rel + [v ^ bit for v in rel]
    odd = jnp.array([v.bit_count() % 2 == 1 for v in rel])[None, :, None, None]
    place = [rel.index(v) for v in range(n_tp)]
    rel, place = jnp.array(rel), jnp.array(place)

    part = tokens
    for bit in bits_of(n_tp):
        part = jnp.concatenate([part, swap(part, bit, 1)])
    part = jnp.stack([part, swap(part, 0, 3)])
    far = swap(part, 0, 1)
    feats = jnp.stack([jnp.where(odd, far, part), jnp.where(odd, part, far)])
    feats = feats.reshape(4 * rows, d_model)
    own = lax.dynamic_slice(feats, (0, r * depth), (4 * rows, depth))

    def partial(weight):
        out = jnp.dot(own, weight, preferred_element_type=F32)
        return (out[: 2 * rows] + swap(out[2 * rows :], 0, 1)).astype(BF16)

    def summed(half):
        other = swap(half, 0, 3)
        other = jnp.concatenate([other[rows:], other[:rows]])
        return half.astype(F32) + other.astype(F32)

    half_gate, half_up = partial(gate_weight), partial(up_weight)
    gate_pre, up_pre = summed(half_gate), summed(half_up)

    cot = swap(cotangent[0], 0, 3)
    near, cot, _ = lax.optimization_barrier((cotangent[0], cot, half_up))
    cot = jnp.stack([near, cot]).reshape(2, n_tp, rt, width)
    cot = jnp.take(cot, t ^ rel, axis=1).reshape(2 * rows, width)

    act, slope = swish_parts(gate_pre)
    hidden = (act * up_pre)[:rows].astype(BF16).reshape(n_tp, rt, width)
    hidden = jnp.take(hidden, place[t ^ jnp.arange(n_tp)], axis=0).reshape(1, rows, width)
    grad_hidden = cot.astype(F32)
    d_gate = (grad_hidden * up_pre * slope).astype(BF16)
    d_up = (grad_hidden * act).astype(BF16)
    d_gate = jnp.concatenate([d_gate, swap(d_gate, 0, 1)])
    d_up = jnp.concatenate([d_up, swap(d_up, 0, 1)])

    cols = (((1,), (1,)), ((), ()))
    total = lax.dot_general(d_gate, gate_weight, cols, preferred_element_type=F32)
    total = total + lax.dot_general(d_up, up_weight, cols, preferred_element_type=F32)
    total = total.reshape(2, 2, n_tp, rt, depth)
    for bit in reversed(bits_of(n_tp)):
        mid = total.shape[2] // 2
        total = total[:, :, :mid] + swap(total[:, :, mid:], bit, 0)
    total = total[:, :, 0]
    total = jnp.stack([total[:, 0], swap(total[:, 1], 0, 3)], axis=1)
    total = jnp.stack([total[0], swap(total[1], 0, 1)])
    total = [total[0, 0], total[1, 0], total[1, 1], total[0, 1]]
    for bit in (1, 2):
        total = [jnp.where(r & bit != 0, total[m ^ bit], total[m]) for m in range(n_dp)]
    grad_tokens = jnp.concatenate([v.astype(BF16) for v in total], axis=1)[None]

    inverse = 1.0 / n_dp
    grad_gate = outer(feats, d_gate, inverse, 0, 2)
    grad_gate = outer(feats, d_gate, inverse, 1, 2, grad_gate)
    grad_up = outer(feats, d_up, inverse, 0, 2)
    grad_up = outer(feats, d_up, inverse, 1, 2, grad_up)
    return hidden, grad_tokens, grad_gate, grad_up


def solution(mesh):
    in_specs = (P("dp", "tp", None), P("dp", "tp"), P("dp", "tp"), P("dp", None, "tp"))
    out_specs = (P("dp", None, "tp"), P("dp", "tp", None), P(None, "tp"), P(None, "tp"))

    return jax.shard_map(shards, mesh=mesh, in_specs=in_specs, out_specs=out_specs, check_vma=False)
```

```python
import functools

import jax
import jax.numpy as jnp
from jax import lax
from jax.experimental import pallas as pl
from jax.experimental.pallas import tpu as pltpu
from jax.sharding import PartitionSpec as P


F32 = jnp.float32
BF16 = jnp.bfloat16
VMEM = pl.BlockSpec(memory_space=pltpu.VMEM)
HBM = pl.BlockSpec(memory_space=pltpu.HBM)
COLS = (((1,), (1,)), ((), ()))
DOWN = (((0,), (0,)), ((), ()))
PIECES = 4


def swap(value, tp_mask, dp_mask):
    n_tp, n_dp = lax.axis_size("tp"), lax.axis_size("dp")
    pairs = [(t * n_dp + r, (t ^ tp_mask) * n_dp + (r ^ dp_mask)) for t in range(n_tp) for r in range(n_dp)]
    return lax.ppermute(value, ("tp", "dp"), pairs)


def bits_of(size):
    assert size & (size - 1) == 0
    return [1 << k for k in reversed(range(size.bit_length() - 1))]


def odd(value):
    return value.bit_count() % 2


def swish_parts(gate_pre):
    s = jax.nn.sigmoid(gate_pre)
    return gate_pre * s, s * (1.0 + gate_pre * (1.0 - s))


def hold_kernel(in_ref, out_ref):
    out_ref[...] = in_ref[...]


def hold(value):
    return pl.pallas_call(
        hold_kernel,
        in_specs=[VMEM],
        out_specs=VMEM,
        out_shape=jax.ShapeDtypeStruct(value.shape, value.dtype),
        compiler_params=pltpu.CompilerParams(vmem_limit_bytes=1 << 20),
        cost_estimate=pl.CostEstimate(flops=0, bytes_accessed=value.size, transcendentals=0),
    )(value)


def pieces_of(weight_ref, buf, sem):
    tall = buf.shape[1]
    return [
        pltpu.make_async_copy(weight_ref.at[pl.ds(i * tall, tall), :], buf.at[i], sem.at[i]) for i in range(PIECES)
    ]


def multiply(feats_ref, copies, buf, keep_ref, send_ref):
    depth = buf.shape[1] * PIECES
    half = keep_ref.shape[0]
    first = lax.axis_index("dp") * depth
    for i, copy in enumerate(copies):
        copy.wait()
        at = pl.multiple_of(first + i * buf.shape[1], buf.shape[1])
        out = jnp.dot(feats_ref[:, pl.ds(at, buf.shape[1])], buf[i], preferred_element_type=F32)
        keep_ref[...] = out[:half] if i == 0 else keep_ref[...] + out[:half]
        send_ref[...] = out[half:] if i == 0 else send_ref[...] + out[half:]


def gather_kernel(part_ref, far_ref, weight_ref, feats_ref, keep_ref, send_ref, buf, sem):
    copies = pieces_of(weight_ref, buf, sem)
    for copy in copies:
        copy.start()
    _, n_tp, rt, _ = part_ref.shape
    for core in range(2):
        for x in range(2):
            for k in range(n_tp):
                source = part_ref if odd(k) == core else far_ref
                row = ((core * 2 + x) * n_tp + k) * rt
                feats_ref[row : row + rt, :] = source[x, k]
    multiply(feats_ref, copies, buf, keep_ref, send_ref)


def ahead_kernel(feats_ref, weight_ref, keep_ref, send_ref, buf, sem):
    copies = pieces_of(weight_ref, buf, sem)
    for copy in copies:
        copy.start()
    multiply(feats_ref, copies, buf, keep_ref, send_ref)


def stream(kernel, args, weight, outs, flops):
    depth, width = weight.shape
    return pl.pallas_call(
        kernel,
        in_specs=[VMEM] * len(args) + [HBM],
        out_specs=[VMEM] * len(outs),
        out_shape=outs,
        scratch_shapes=[pltpu.VMEM((PIECES, depth // PIECES, width), BF16), pltpu.SemaphoreType.DMA((PIECES,))],
        compiler_params=pltpu.CompilerParams(vmem_limit_bytes=52 << 20),
        cost_estimate=pl.CostEstimate(flops=flops, bytes_accessed=2 * weight.size, transcendentals=0),
    )(*args, weight)


def gather_ahead(part, far, weight):
    _, n_tp, rt, d_model = part.shape
    count, width = 4 * n_tp * rt, weight.shape[1]
    half = jax.ShapeDtypeStruct((count // 2, width), F32)
    if n_tp <= 16:
        feats = jax.ShapeDtypeStruct((count, d_model), BF16)
        return stream(gather_kernel, (part, far), weight, [feats, half, half], 2 * count * weight.size)
    mask = jnp.array([odd(k) == 1 for k in range(n_tp)])[None, :, None, None]
    feats = jnp.stack([jnp.where(mask, far, part), jnp.where(mask, part, far)]).reshape(count, d_model)
    return feats, *ahead(feats, weight)


def ahead(feats, weight):
    half = jax.ShapeDtypeStruct((feats.shape[0] // 2, weight.shape[1]), F32)
    return stream(ahead_kernel, (feats,), weight, [half, half], 2 * feats.shape[0] * weight.size)


def back_kernel(*refs):
    grad_ref, weight_ref, out_ref, buf, sem = refs[0], *refs[-4:]
    copies = pieces_of(weight_ref, buf, sem)
    for copy in copies:
        copy.start()
    tall = buf.shape[1]
    for i, copy in enumerate(copies):
        copy.wait()
        out = lax.dot_general(grad_ref[...], buf[i], COLS, preferred_element_type=F32)
        at = slice(i * tall, (i + 1) * tall)
        out_ref[:, at] = out if len(refs) == 5 else refs[1][:, at] + out


def back(grad, weight, start=None):
    out = jax.ShapeDtypeStruct((grad.shape[0], weight.shape[0]), F32)
    args = (grad,) if start is None else (grad, start)
    return stream(back_kernel, args, weight, [out], 2 * grad.shape[0] * weight.size)[0]


def outer_kernel(rows_ref, grad_ref, *rest, base, scale):
    out_ref, buf, sem = rest[-3:]
    total, width = buf.shape
    wide = min(512, width)
    tall = min(512, total)
    sizes = [tall // 2] * 2 + [tall] * (total // tall - 1)
    copies = []
    top = 0
    for i, size in enumerate(sizes):
        for at in range(0, width, wide):
            acc = lax.dot_general(
                rows_ref[:, base + top : base + top + size],
                grad_ref[:, at : at + wide],
                DOWN,
                preferred_element_type=F32,
            )
            buf[top : top + size, at : at + wide] = (acc * scale).astype(BF16)
        source, target = buf.at[pl.ds(top, size), :], out_ref.at[pl.ds(base + top, size), :]
        copies.append(pltpu.make_async_copy(source, target, sem.at[i]))
        copies[-1].start()
        top += size
    for copy in copies:
        copy.wait()


def outer(rows, grad, scale, begin, share, whole=None):
    count, d_model = rows.shape
    width = grad.shape[1]
    part = d_model // share
    kernel = functools.partial(outer_kernel, base=begin * part, scale=scale)
    args = (rows, grad) if whole is None else (rows, grad, whole)
    return pl.pallas_call(
        kernel,
        in_specs=[VMEM, VMEM] + [HBM] * (len(args) - 2),
        out_specs=HBM,
        out_shape=jax.ShapeDtypeStruct((d_model, width), BF16),
        input_output_aliases={2: 0} if whole is not None else {},
        scratch_shapes=[pltpu.VMEM((part, width), BF16), pltpu.SemaphoreType.DMA((part // min(512, part) + 1,))],
        compiler_params=pltpu.CompilerParams(vmem_limit_bytes=32 << 20),
        cost_estimate=pl.CostEstimate(
            flops=2 * count * part * width,
            bytes_accessed=2 * part * width + 2 * count * (d_model + width),
            transcendentals=0,
        ),
    )(*args)


def shards(tokens, gate_weight, up_weight, cotangent):
    n_tp, n_dp = lax.axis_size("tp"), lax.axis_size("dp")
    assert n_dp == 4
    t, r = lax.axis_index("tp"), lax.axis_index("dp")
    _, rt, d_model = tokens.shape
    depth, width = gate_weight.shape
    rows = rt * n_tp
    order = t ^ jnp.arange(n_tp)

    part = hold(tokens)
    for i, bit in enumerate(bits_of(n_tp)):
        near = swap(part if i else tokens, bit, 1)
        part = jnp.stack([part, near], axis=1).reshape(-1, rt, d_model)
    part = jnp.stack([part, swap(part, 0, 3)])
    far = swap(part, 0, 1)
    feats, gate_keep, gate_send = gather_ahead(part, far, gate_weight)
    up_keep, up_send = ahead(feats, up_weight)

    def partial(keep, send):
        return (keep + swap(send, 0, 1)).astype(BF16)

    def summed(half):
        other = swap(half, 0, 3)
        other = jnp.concatenate([other[rows:], other[:rows]])
        return half.astype(F32) + other.astype(F32)

    half_gate, half_up = partial(gate_keep, gate_send), partial(up_keep, up_send)
    gate_pre = summed(half_gate)
    up_pre = summed(half_up)

    cot = swap(cotangent[0], 0, 3)
    near, cot, _ = lax.optimization_barrier((cotangent[0], cot, half_up))
    cot = jnp.stack([near, cot]).reshape(2, n_tp, rt, width)
    cot = jnp.take(cot, order, axis=1).reshape(2 * rows, width)

    act, slope = swish_parts(gate_pre)
    grad_hidden = cot.astype(F32)
    d_up = (grad_hidden * act).astype(BF16)
    d_up, act, slope = lax.optimization_barrier((d_up, act, slope))
    d_up = jnp.concatenate([d_up, swap(d_up, 0, 1)])
    total = back(d_up, up_weight)
    hidden = (act * up_pre)[:rows].astype(BF16).reshape(n_tp, rt, width)
    hidden = jnp.take(hidden, order, axis=0).reshape(1, rows, width)
    d_gate = (grad_hidden * up_pre * slope).astype(BF16)
    d_gate = jnp.concatenate([d_gate, swap(d_gate, 0, 1)])
    total = back(d_gate, gate_weight, total)

    total = total.reshape(2, 2, n_tp, rt, depth)
    for bit in reversed(bits_of(n_tp)):
        total = total.reshape(2, 2, -1, 2, rt, depth)
        total = total[:, :, :, 0] + swap(total[:, :, :, 1], bit, 0)
    total = total[:, :, 0]
    total = jnp.stack([total[:, 0], swap(total[:, 1], 0, 3)], axis=1)
    total = jnp.stack([total[0], swap(total[1], 0, 1)])
    total = [total[0, 0], total[1, 0], total[1, 1], total[0, 1]]
    for bit in (1, 2):
        total = [jnp.where(r & bit != 0, total[m ^ bit], total[m]) for m in range(n_dp)]
    grad_tokens = jnp.concatenate([v.astype(BF16) for v in total], axis=1)[None]

    inverse = 1.0 / n_dp
    grad_up = outer(feats, d_up, inverse, 0, 2)
    grad_up = outer(feats, d_up, inverse, 1, 2, grad_up)
    grad_gate = outer(feats, d_gate, inverse, 0, 2)
    grad_gate = outer(feats, d_gate, inverse, 1, 2, grad_gate)
    return hidden, grad_tokens, grad_gate, grad_up


def solution(mesh):
    in_specs = (P("dp", "tp", None), P("dp", "tp"), P("dp", "tp"), P("dp", None, "tp"))
    out_specs = (P("dp", None, "tp"), P("dp", "tp", None), P(None, "tp"), P(None, "tp"))

    return jax.shard_map(shards, mesh=mesh, in_specs=in_specs, out_specs=out_specs, check_vma=False)
```

```python
import functools

import jax
import jax.numpy as jnp
from jax import lax
from jax.experimental import pallas as pl
from jax.experimental.pallas import tpu as pltpu
from jax.sharding import PartitionSpec as P


F32 = jnp.float32
BF16 = jnp.bfloat16
VMEM = pl.BlockSpec(memory_space=pltpu.VMEM)
HBM = pl.BlockSpec(memory_space=pltpu.HBM)
COLS = (((1,), (1,)), ((), ()))
DOWN = (((0,), (0,)), ((), ()))
PIECES = 4


def swap(value, tp_mask, dp_mask):
    n_tp, n_dp = lax.axis_size("tp"), lax.axis_size("dp")
    pairs = [(t * n_dp + r, (t ^ tp_mask) * n_dp + (r ^ dp_mask)) for t in range(n_tp) for r in range(n_dp)]
    return lax.ppermute(value, ("tp", "dp"), pairs)


def bits_of(size):
    assert size & (size - 1) == 0
    return [1 << k for k in reversed(range(size.bit_length() - 1))]


def odd(value):
    return value.bit_count() % 2


def swish_parts(gate_pre):
    s = jax.nn.sigmoid(gate_pre)
    return gate_pre * s, s * (1.0 + gate_pre * (1.0 - s))


def hold_kernel(in_ref, out_ref):
    out_ref[...] = in_ref[...]


def hold(value):
    return pl.pallas_call(
        hold_kernel,
        in_specs=[VMEM],
        out_specs=VMEM,
        out_shape=jax.ShapeDtypeStruct(value.shape, value.dtype),
        compiler_params=pltpu.CompilerParams(vmem_limit_bytes=1 << 20),
        cost_estimate=pl.CostEstimate(flops=0, bytes_accessed=value.size, transcendentals=0),
    )(value)


def pieces_of(weight_ref, buf, sem):
    tall = buf.shape[1]
    return [
        pltpu.make_async_copy(weight_ref.at[pl.ds(i * tall, tall), :], buf.at[i], sem.at[i]) for i in range(PIECES)
    ]


def multiply(feats_ref, copies, buf, keep_ref, send_ref):
    depth = buf.shape[1] * PIECES
    half = keep_ref.shape[0]
    first = lax.axis_index("dp") * depth
    for i, copy in enumerate(copies):
        copy.wait()
        at = pl.multiple_of(first + i * buf.shape[1], buf.shape[1])
        out = jnp.dot(feats_ref[:, pl.ds(at, buf.shape[1])], buf[i], preferred_element_type=F32)
        keep_ref[...] = out[:half] if i == 0 else keep_ref[...] + out[:half]
        send_ref[...] = out[half:] if i == 0 else send_ref[...] + out[half:]


def gather_kernel(part_ref, far_ref, weight_ref, feats_ref, keep_ref, send_ref, buf, sem):
    copies = pieces_of(weight_ref, buf, sem)
    for copy in copies:
        copy.start()
    _, n_tp, rt, _ = part_ref.shape
    for core in range(2):
        for x in range(2):
            for k in range(n_tp):
                source = part_ref if odd(k) == core else far_ref
                row = ((core * 2 + x) * n_tp + k) * rt
                feats_ref[row : row + rt, :] = source[x, k]
    multiply(feats_ref, copies, buf, keep_ref, send_ref)


def ahead_kernel(feats_ref, weight_ref, keep_ref, send_ref, buf, sem):
    copies = pieces_of(weight_ref, buf, sem)
    for copy in copies:
        copy.start()
    multiply(feats_ref, copies, buf, keep_ref, send_ref)


def stream(kernel, args, weight, outs, flops, pieces=None):
    depth, width = weight.shape
    pieces = pieces or (PIECES, depth // PIECES, width)
    return pl.pallas_call(
        kernel,
        in_specs=[VMEM] * len(args) + [HBM],
        out_specs=[VMEM] * len(outs),
        out_shape=outs,
        scratch_shapes=[pltpu.VMEM(pieces, BF16), pltpu.SemaphoreType.DMA((pieces[0],))],
        compiler_params=pltpu.CompilerParams(vmem_limit_bytes=52 << 20),
        cost_estimate=pl.CostEstimate(flops=flops, bytes_accessed=2 * weight.size, transcendentals=0),
    )(*args, weight)


def gather_ahead(part, far, weight):
    _, n_tp, rt, d_model = part.shape
    count, width = 4 * n_tp * rt, weight.shape[1]
    half = jax.ShapeDtypeStruct((count // 2, width), F32)
    if n_tp <= 16:
        feats = jax.ShapeDtypeStruct((count, d_model), BF16)
        return stream(gather_kernel, (part, far), weight, [feats, half, half], 2 * count * weight.size)
    mask = jnp.array([odd(k) == 1 for k in range(n_tp)])[None, :, None, None]
    feats = jnp.stack([jnp.where(mask, far, part), jnp.where(mask, part, far)]).reshape(count, d_model)
    return feats, *ahead(feats, weight)


def ahead(feats, weight):
    half = jax.ShapeDtypeStruct((feats.shape[0] // 2, weight.shape[1]), F32)
    return stream(ahead_kernel, (feats,), weight, [half, half], 2 * feats.shape[0] * weight.size)


def back_kernel(*refs):
    grad_ref, weight_ref, out_ref, buf, sem = refs[0], *refs[-4:]
    count, _, wide = buf.shape
    parts = [pl.ds(i * wide, wide) for i in range(count)]
    copies = [pltpu.make_async_copy(weight_ref.at[:, at], buf.at[i], sem.at[i]) for i, at in enumerate(parts)]
    for copy in copies:
        copy.start()
    for i, copy in enumerate(copies):
        copy.wait()
        out = lax.dot_general(grad_ref[:, parts[i]], buf[i], COLS, preferred_element_type=F32)
        if i:
            out_ref[...] += out
        else:
            out_ref[...] = out if len(refs) == 5 else refs[1][...] + out


def back(grad, weight, start=None):
    depth, width = weight.shape
    pieces = PIECES if width % (128 * PIECES) == 0 else 1
    out = jax.ShapeDtypeStruct((grad.shape[0], depth), F32)
    args = (grad,) if start is None else (grad, start)
    return stream(back_kernel, args, weight, [out], 2 * grad.shape[0] * weight.size, (pieces, depth, width // pieces))[0]


def outer_kernel(rows_ref, grad_ref, *rest, base, scale):
    out_ref, buf, sem = rest[-3:]
    total, width = buf.shape
    wide = min(512, width)
    tall = min(512, total)
    sizes = [tall // 2] * 2 + [tall] * (total // tall - 1)
    copies = []
    top = 0
    for i, size in enumerate(sizes):
        for at in range(0, width, wide):
            acc = lax.dot_general(
                rows_ref[:, base + top : base + top + size],
                grad_ref[:, at : at + wide],
                DOWN,
                preferred_element_type=F32,
            )
            buf[top : top + size, at : at + wide] = (acc * scale).astype(BF16)
        source, target = buf.at[pl.ds(top, size), :], out_ref.at[pl.ds(base + top, size), :]
        copies.append(pltpu.make_async_copy(source, target, sem.at[i]))
        copies[-1].start()
        top += size
    for copy in copies:
        copy.wait()


def outer(rows, grad, scale, begin, share, whole=None):
    count, d_model = rows.shape
    width = grad.shape[1]
    part = d_model // share
    kernel = functools.partial(outer_kernel, base=begin * part, scale=scale)
    args = (rows, grad) if whole is None else (rows, grad, whole)
    return pl.pallas_call(
        kernel,
        in_specs=[VMEM, VMEM] + [HBM] * (len(args) - 2),
        out_specs=HBM,
        out_shape=jax.ShapeDtypeStruct((d_model, width), BF16),
        input_output_aliases={2: 0} if whole is not None else {},
        scratch_shapes=[pltpu.VMEM((part, width), BF16), pltpu.SemaphoreType.DMA((part // min(512, part) + 1,))],
        compiler_params=pltpu.CompilerParams(vmem_limit_bytes=32 << 20),
        cost_estimate=pl.CostEstimate(
            flops=2 * count * part * width,
            bytes_accessed=2 * part * width + 2 * count * (d_model + width),
            transcendentals=0,
        ),
    )(*args)


def shards(tokens, gate_weight, up_weight, cotangent):
    n_tp, n_dp = lax.axis_size("tp"), lax.axis_size("dp")
    assert n_dp == 4
    t, r = lax.axis_index("tp"), lax.axis_index("dp")
    _, rt, d_model = tokens.shape
    depth, width = gate_weight.shape
    rows = rt * n_tp
    order = t ^ jnp.arange(n_tp)

    part = hold(tokens)
    for i, bit in enumerate(bits_of(n_tp)):
        near = swap(part if i else tokens, bit, 1)
        part = jnp.stack([part, near], axis=1).reshape(-1, rt, d_model)
    part = jnp.stack([part, swap(part, 0, 3)])
    far = swap(part, 0, 1)
    feats, gate_keep, gate_send = gather_ahead(part, far, gate_weight)
    up_keep, up_send = ahead(feats, up_weight)

    def partial(keep, send):
        other = swap(send, 0, 1)
        return (keep + other).astype(BF16)

    def summed(half):
        other = swap(half, 0, 3)
        other = jnp.concatenate([other[rows:], other[:rows]])
        return half.astype(F32) + other.astype(F32)

    half_gate = partial(gate_keep, gate_send)
    half_up = partial(up_keep, up_send)
    gate_pre = summed(half_gate)
    up_pre = summed(half_up)

    cot = swap(cotangent[0], 0, 3)
    near, cot, _ = lax.optimization_barrier((cotangent[0], cot, up_keep))
    cot = jnp.stack([near, cot]).reshape(2, n_tp, rt, width)
    cot = jnp.take(cot, order, axis=1).reshape(2 * rows, width)

    grad_hidden = cot.astype(F32)
    act, slope = swish_parts(gate_pre)
    d_up = (grad_hidden * act).astype(BF16)
    d_up, act, slope = lax.optimization_barrier((d_up, act, slope))
    far = swap(d_up, 0, 1)
    d_up = jnp.concatenate([d_up, far])
    total = back(d_up, up_weight)
    hidden = (act * up_pre)[:rows].astype(BF16).reshape(n_tp, rt, width)
    hidden = jnp.take(hidden, order, axis=0).reshape(1, rows, width)
    d_gate = (grad_hidden * up_pre * slope).astype(BF16)
    far = swap(d_gate, 0, 1)
    d_gate = jnp.concatenate([d_gate, far])
    total = back(d_gate, gate_weight, total)

    total = total.reshape(2, 2, n_tp, rt, depth)
    for bit in reversed(bits_of(n_tp)):
        total = total.reshape(2, 2, -1, 2, rt, depth)
        total = total[:, :, :, 0] + swap(total[:, :, :, 1], bit, 0)
    total = total[:, :, 0]
    total = jnp.stack([total[:, 0], swap(total[:, 1], 0, 3)], axis=1)
    total = jnp.stack([total[0], swap(total[1], 0, 1)])
    total = [total[0, 0], total[1, 0], total[1, 1], total[0, 1]]
    for bit in (1, 2):
        total = [jnp.where(r & bit != 0, total[m ^ bit], total[m]) for m in range(n_dp)]
    grad_tokens = jnp.concatenate([v.astype(BF16) for v in total], axis=1)[None]

    inverse = 1.0 / n_dp
    grad_up = outer(feats, d_up, inverse, 0, 2)
    grad_up = outer(feats, d_up, inverse, 1, 2, grad_up)
    grad_gate = outer(feats, d_gate, inverse, 0, 2)
    grad_gate = outer(feats, d_gate, inverse, 1, 2, grad_gate)
    return hidden, grad_tokens, grad_gate, grad_up


def solution(mesh):
    in_specs = (P("dp", "tp", None), P("dp", "tp"), P("dp", "tp"), P("dp", None, "tp"))
    out_specs = (P("dp", None, "tp"), P("dp", "tp", None), P(None, "tp"), P(None, "tp"))

    return jax.shard_map(shards, mesh=mesh, in_specs=in_specs, out_specs=out_specs, check_vma=False)
```

```python
import functools

import jax
import jax.numpy as jnp
from jax import lax
from jax.experimental import pallas as pl
from jax.experimental.pallas import tpu as pltpu
from jax.sharding import PartitionSpec as P


F32 = jnp.float32
BF16 = jnp.bfloat16
VMEM = pl.BlockSpec(memory_space=pltpu.VMEM)
HBM = pl.BlockSpec(memory_space=pltpu.HBM)
COLS = (((1,), (1,)), ((), ()))
DOWN = (((0,), (0,)), ((), ()))
PIECES = 4


def swap(value, tp_mask, dp_mask):
    n_tp, n_dp = lax.axis_size("tp"), lax.axis_size("dp")
    pairs = [(t * n_dp + r, (t ^ tp_mask) * n_dp + (r ^ dp_mask)) for t in range(n_tp) for r in range(n_dp)]
    return lax.ppermute(value, ("tp", "dp"), pairs)


def bits_of(size):
    assert size & (size - 1) == 0
    return [1 << k for k in reversed(range(size.bit_length() - 1))]


def odd(value):
    return value.bit_count() % 2


def swish_parts(gate_pre):
    s = jax.nn.sigmoid(gate_pre)
    return gate_pre * s, s * (1.0 + gate_pre * (1.0 - s))


def hold_kernel(in_ref, out_ref):
    out_ref[...] = in_ref[...]


def hold(value):
    return pl.pallas_call(
        hold_kernel,
        in_specs=[VMEM],
        out_specs=VMEM,
        out_shape=jax.ShapeDtypeStruct(value.shape, value.dtype),
        compiler_params=pltpu.CompilerParams(vmem_limit_bytes=1 << 20),
        cost_estimate=pl.CostEstimate(flops=0, bytes_accessed=value.size, transcendentals=0),
    )(value)


def pieces_of(weight_ref, buf, sem):
    tall = buf.shape[1]
    return [
        pltpu.make_async_copy(weight_ref.at[pl.ds(i * tall, tall), :], buf.at[i], sem.at[i]) for i in range(PIECES)
    ]


def multiply(feats_ref, copies, buf, keep_ref, send_ref):
    depth = buf.shape[1] * PIECES
    half = keep_ref.shape[0]
    first = lax.axis_index("dp") * depth
    for i, copy in enumerate(copies):
        copy.wait()
        at = pl.multiple_of(first + i * buf.shape[1], buf.shape[1])
        out = jnp.dot(feats_ref[:, pl.ds(at, buf.shape[1])], buf[i], preferred_element_type=F32)
        keep_ref[...] = out[:half] if i == 0 else keep_ref[...] + out[:half]
        send_ref[...] = out[half:] if i == 0 else send_ref[...] + out[half:]


def gather_kernel(part_ref, far_ref, weight_ref, feats_ref, keep_ref, send_ref, buf, sem):
    copies = pieces_of(weight_ref, buf, sem)
    for copy in copies:
        copy.start()
    _, n_tp, rt, _ = part_ref.shape
    for core in range(2):
        for x in range(2):
            for k in range(n_tp):
                source = part_ref if odd(k) == core else far_ref
                row = ((core * 2 + x) * n_tp + k) * rt
                feats_ref[row : row + rt, :] = source[x, k]
    multiply(feats_ref, copies, buf, keep_ref, send_ref)


def ahead_kernel(feats_ref, weight_ref, keep_ref, send_ref, buf, sem):
    copies = pieces_of(weight_ref, buf, sem)
    for copy in copies:
        copy.start()
    multiply(feats_ref, copies, buf, keep_ref, send_ref)


def stream(kernel, args, weight, outs, flops, pieces=None):
    depth, width = weight.shape
    pieces = pieces or (PIECES, depth // PIECES, width)
    return pl.pallas_call(
        kernel,
        in_specs=[VMEM] * len(args) + [HBM],
        out_specs=[VMEM] * len(outs),
        out_shape=outs,
        scratch_shapes=[pltpu.VMEM(pieces, BF16), pltpu.SemaphoreType.DMA((pieces[0],))],
        compiler_params=pltpu.CompilerParams(vmem_limit_bytes=52 << 20),
        cost_estimate=pl.CostEstimate(flops=flops, bytes_accessed=2 * weight.size, transcendentals=0),
    )(*args, weight)


def gather_ahead(part, far, weight):
    _, n_tp, rt, d_model = part.shape
    count, width = 4 * n_tp * rt, weight.shape[1]
    half = jax.ShapeDtypeStruct((count // 2, width), F32)
    if n_tp <= 16:
        feats = jax.ShapeDtypeStruct((count, d_model), BF16)
        return stream(gather_kernel, (part, far), weight, [feats, half, half], 2 * count * weight.size)
    mask = jnp.array([odd(k) == 1 for k in range(n_tp)])[None, :, None, None]
    feats = jnp.stack([jnp.where(mask, far, part), jnp.where(mask, part, far)]).reshape(count, d_model)
    return feats, *ahead(feats, weight)


def ahead(feats, weight):
    half = jax.ShapeDtypeStruct((feats.shape[0] // 2, weight.shape[1]), F32)
    return stream(ahead_kernel, (feats,), weight, [half, half], 2 * feats.shape[0] * weight.size)


def back_kernel(*refs):
    grad_ref, weight_ref, out_ref, buf, sem = refs[0], *refs[-4:]
    count, _, wide = buf.shape
    parts = [pl.ds(i * wide, wide) for i in range(count)]
    copies = [pltpu.make_async_copy(weight_ref.at[:, at], buf.at[i], sem.at[i]) for i, at in enumerate(parts)]
    for copy in copies:
        copy.start()
    for i, copy in enumerate(copies):
        copy.wait()
        out = lax.dot_general(grad_ref[:, parts[i]], buf[i], COLS, preferred_element_type=F32)
        if i:
            out_ref[...] += out
        else:
            out_ref[...] = out if len(refs) == 5 else refs[1][...] + out


def back(grad, weight, start=None):
    depth, width = weight.shape
    pieces = PIECES if width % (128 * PIECES) == 0 else 1
    out = jax.ShapeDtypeStruct((grad.shape[0], depth), F32)
    args = (grad,) if start is None else (grad, start)
    return stream(back_kernel, args, weight, [out], 2 * grad.shape[0] * weight.size, (pieces, depth, width // pieces))[0]


def outer_kernel(rows_ref, grad_ref, *rest, base, scale):
    out_ref, buf, sem = rest[-3:]
    total, width = buf.shape
    wide = min(512, width)
    tall = min(512, total)
    sizes = [tall // 2] * 2 + [tall] * (total // tall - 1)
    copies = []
    top = 0
    for i, size in enumerate(sizes):
        for at in range(0, width, wide):
            acc = lax.dot_general(
                rows_ref[:, base + top : base + top + size],
                grad_ref[:, at : at + wide],
                DOWN,
                preferred_element_type=F32,
            )
            buf[top : top + size, at : at + wide] = (acc * scale).astype(BF16)
        source, target = buf.at[pl.ds(top, size), :], out_ref.at[pl.ds(base + top, size), :]
        copies.append(pltpu.make_async_copy(source, target, sem.at[i]))
        copies[-1].start()
        top += size
    for copy in copies:
        copy.wait()


def outer(rows, grad, scale, begin, share, whole=None):
    count, d_model = rows.shape
    width = grad.shape[1]
    part = d_model // share
    kernel = functools.partial(outer_kernel, base=begin * part, scale=scale)
    args = (rows, grad) if whole is None else (rows, grad, whole)
    return pl.pallas_call(
        kernel,
        in_specs=[VMEM, VMEM] + [HBM] * (len(args) - 2),
        out_specs=HBM,
        out_shape=jax.ShapeDtypeStruct((d_model, width), BF16),
        input_output_aliases={2: 0} if whole is not None else {},
        scratch_shapes=[pltpu.VMEM((part, width), BF16), pltpu.SemaphoreType.DMA((part // min(512, part) + 1,))],
        compiler_params=pltpu.CompilerParams(vmem_limit_bytes=32 << 20),
        cost_estimate=pl.CostEstimate(
            flops=2 * count * part * width,
            bytes_accessed=2 * part * width + 2 * count * (d_model + width),
            transcendentals=0,
        ),
    )(*args)


def shards(tokens, gate_weight, up_weight, cotangent):
    n_tp, n_dp = lax.axis_size("tp"), lax.axis_size("dp")
    assert n_dp == 4
    t, r = lax.axis_index("tp"), lax.axis_index("dp")
    _, rt, d_model = tokens.shape
    depth, width = gate_weight.shape
    rows = rt * n_tp
    order = t ^ jnp.arange(n_tp)

    part = hold(tokens)
    for i, bit in enumerate(bits_of(n_tp)):
        near = swap(part if i else tokens, bit, 1)
        part = jnp.stack([part, near], axis=1).reshape(-1, rt, d_model)
    part = jnp.stack([part, swap(part, 0, 3)])
    far = swap(part, 0, 1)
    feats, gate_keep, gate_send = gather_ahead(part, far, gate_weight)
    up_keep, up_send = ahead(feats, up_weight)

    def partial(keep, send):
        other = swap(send, 0, 1)
        return (keep + other).astype(BF16)

    def summed(half):
        other = swap(half, 0, 3)
        other = jnp.concatenate([other[rows:], other[:rows]])
        return half.astype(F32) + other.astype(F32)

    half_gate = partial(gate_keep, gate_send)
    half_up = partial(up_keep, up_send)
    gate_pre = summed(half_gate)
    up_pre = summed(half_up)

    cot = swap(cotangent[0], 0, 3)
    cot = jnp.stack([cotangent[0], cot]).reshape(2, n_tp, rt, width)
    cot = jnp.take(cot, order, axis=1).reshape(2 * rows, width)

    grad_hidden = cot.astype(F32)
    act, slope = swish_parts(gate_pre)
    d_up = (grad_hidden * act).astype(BF16)
    d_up, act, slope = lax.optimization_barrier((d_up, act, slope))
    far = swap(d_up, 0, 1)
    d_up = jnp.concatenate([d_up, far])
    total = back(d_up, up_weight)
    hidden = (act * up_pre)[:rows].astype(BF16).reshape(n_tp, rt, width)
    hidden = jnp.take(hidden, order, axis=0).reshape(1, rows, width)
    d_gate = (grad_hidden * up_pre * slope).astype(BF16)
    far = swap(d_gate, 0, 1)
    d_gate = jnp.concatenate([d_gate, far])
    total = back(d_gate, gate_weight, total)

    total = total.reshape(2, 2, n_tp, rt, depth)
    for bit in reversed(bits_of(n_tp)):
        total = total.reshape(2, 2, -1, 2, rt, depth)
        total = total[:, :, :, 0] + swap(total[:, :, :, 1], bit, 0)
    total = total[:, :, 0]
    total = jnp.stack([total[:, 0], swap(total[:, 1], 0, 3)], axis=1)
    total = jnp.stack([total[0], swap(total[1], 0, 1)])
    total = [total[0, 0], total[1, 0], total[1, 1], total[0, 1]]
    for bit in (1, 2):
        total = [jnp.where(r & bit != 0, total[m ^ bit], total[m]) for m in range(n_dp)]
    grad_tokens = jnp.concatenate([v.astype(BF16) for v in total], axis=1)[None]

    inverse = 1.0 / n_dp
    grad_up = outer(feats, d_up, inverse, 0, 2)
    grad_up = outer(feats, d_up, inverse, 1, 2, grad_up)
    grad_gate = outer(feats, d_gate, inverse, 0, 2)
    grad_gate = outer(feats, d_gate, inverse, 2, 4, grad_gate)
    grad_gate = outer(feats, d_gate, inverse, 3, 4, grad_gate)
    return hidden, grad_tokens, grad_gate, grad_up


def solution(mesh):
    in_specs = (P("dp", "tp", None), P("dp", "tp"), P("dp", "tp"), P("dp", None, "tp"))
    out_specs = (P("dp", None, "tp"), P("dp", "tp", None), P(None, "tp"), P(None, "tp"))

    return jax.shard_map(shards, mesh=mesh, in_specs=in_specs, out_specs=out_specs, check_vma=False)
```

```python
import functools

import jax
import jax.numpy as jnp
from jax import lax
from jax.experimental import pallas as pl
from jax.experimental.pallas import tpu as pltpu
from jax.sharding import PartitionSpec as P


F32 = jnp.float32
BF16 = jnp.bfloat16
VMEM = pl.BlockSpec(memory_space=pltpu.VMEM)
HBM = pl.BlockSpec(memory_space=pltpu.HBM)
COLS = (((1,), (1,)), ((), ()))
DOWN = (((0,), (0,)), ((), ()))
PIECES = 4


def swap(value, tp_mask, dp_mask):
    n_tp, n_dp = lax.axis_size("tp"), lax.axis_size("dp")
    pairs = [(t * n_dp + r, (t ^ tp_mask) * n_dp + (r ^ dp_mask)) for t in range(n_tp) for r in range(n_dp)]
    return lax.ppermute(value, ("tp", "dp"), pairs)


def bits_of(size):
    assert size & (size - 1) == 0
    return [1 << k for k in reversed(range(size.bit_length() - 1))]


def odd(value):
    return value.bit_count() % 2


def swish_parts(gate_pre):
    s = jax.nn.sigmoid(gate_pre)
    return gate_pre * s, s * (1.0 + gate_pre * (1.0 - s))


def hold_kernel(in_ref, out_ref):
    out_ref[...] = in_ref[...]


def hold(value):
    return pl.pallas_call(
        hold_kernel,
        in_specs=[VMEM],
        out_specs=VMEM,
        out_shape=jax.ShapeDtypeStruct(value.shape, value.dtype),
        compiler_params=pltpu.CompilerParams(vmem_limit_bytes=1 << 20),
        cost_estimate=pl.CostEstimate(flops=0, bytes_accessed=value.size, transcendentals=0),
    )(value)


def reorder_kernel(in_ref, out_ref, *, rt):
    rows = in_ref.shape[0]
    to = lax.broadcasted_iota(jnp.int32, (rows, rows), 0)
    source = lax.broadcasted_iota(jnp.int32, (rows, rows), 1)
    pick = ((to ^ (lax.axis_index("tp") * rt)) == source).astype(F32).astype(BF16)
    out_ref[...] = jnp.dot(pick, in_ref[...], preferred_element_type=F32).astype(BF16)


def reorder(value, rt):
    assert rt & (rt - 1) == 0
    return pl.pallas_call(
        functools.partial(reorder_kernel, rt=rt),
        in_specs=[VMEM],
        out_specs=VMEM,
        out_shape=jax.ShapeDtypeStruct(value.shape, BF16),
        compiler_params=pltpu.CompilerParams(vmem_limit_bytes=8 << 20),
        cost_estimate=pl.CostEstimate(flops=0, bytes_accessed=4 * value.size, transcendentals=0),
    )(value)


def load_kernel(weight_ref, out_ref, sem, *, begin):
    tall = out_ref.shape[0] // 2
    copies = [
        pltpu.make_async_copy(
            weight_ref.at[pl.ds(begin + i * tall, tall), :], out_ref.at[pl.ds(i * tall, tall), :], sem.at[i]
        )
        for i in range(2)
    ]
    for copy in copies:
        copy.start()
    for copy in copies:
        copy.wait()


def load(weight, part, parts):
    depth, width = weight.shape
    depth //= parts
    return pl.pallas_call(
        functools.partial(load_kernel, begin=part * depth),
        in_specs=[HBM],
        out_specs=VMEM,
        out_shape=jax.ShapeDtypeStruct((depth, width), BF16),
        scratch_shapes=[pltpu.SemaphoreType.DMA((2,))],
        compiler_params=pltpu.CompilerParams(vmem_limit_bytes=48 << 20),
        cost_estimate=pl.CostEstimate(flops=0, bytes_accessed=2 * depth * width, transcendentals=0),
    )(weight)


def add_product(feats_ref, at, weight, keep_ref, send_ref):
    half = keep_ref.shape[0]
    start = pl.multiple_of(lax.axis_index("dp") * at[1] + at[0], weight.shape[0])
    out = jnp.dot(feats_ref[:, pl.ds(start, weight.shape[0])], weight, preferred_element_type=F32)
    if at[0]:
        keep_ref[...] += out[:half]
        send_ref[...] += out[half:]
    else:
        keep_ref[...] = out[:half]
        send_ref[...] = out[half:]


def stream_product(feats_ref, copies, held_ref, keep_ref, send_ref):
    depth = held_ref.shape[0]
    tall = depth // PIECES
    for i, copy in enumerate(copies):
        copy.wait()
        add_product(feats_ref, (i * tall, depth), held_ref[i * tall : (i + 1) * tall, :], keep_ref, send_ref)


def start_copies(weight_ref, held_ref, sem):
    tall = held_ref.shape[0] // PIECES
    parts = [pl.ds(i * tall, tall) for i in range(PIECES)]
    copies = [
        pltpu.make_async_copy(weight_ref.at[at, :], held_ref.at[at, :], sem.at[i]) for i, at in enumerate(parts)
    ]
    for copy in copies:
        copy.start()
    return copies


def gather_kernel(part_ref, far_ref, weight_ref, held_ref, keep_ref, send_ref, feats_ref, sem):
    copies = start_copies(weight_ref, held_ref, sem)
    _, n_tp, rt, _ = part_ref.shape
    for core in range(2):
        for x in range(2):
            for k in range(n_tp):
                source = part_ref if odd(k) == core else far_ref
                row = ((core * 2 + x) * n_tp + k) * rt
                feats_ref[row : row + rt, :] = source[x, k]
    stream_product(feats_ref, copies, held_ref, keep_ref, send_ref)


def stream_kernel(feats_ref, weight_ref, held_ref, keep_ref, send_ref, sem):
    copies = start_copies(weight_ref, held_ref, sem)
    stream_product(feats_ref, copies, held_ref, keep_ref, send_ref)


def gather_ahead(part, far, weight):
    _, n_tp, rt, d_model = part.shape
    count, width = 4 * n_tp * rt, weight.shape[1]
    half = jax.ShapeDtypeStruct((count // 2, width), F32)
    outs = [jax.ShapeDtypeStruct(weight.shape, BF16), half, half]
    if n_tp <= 16:
        outs.append(jax.ShapeDtypeStruct((count, d_model), BF16))
        kernel, args = gather_kernel, (part, far, weight)
    else:
        mask = jnp.array([odd(k) == 1 for k in range(n_tp)])[None, :, None, None]
        feats = jnp.stack([jnp.where(mask, far, part), jnp.where(mask, part, far)]).reshape(count, d_model)
        kernel, args = stream_kernel, (feats, weight)
    held, keep, send, *rest = pl.pallas_call(
        kernel,
        in_specs=[VMEM] * (len(args) - 1) + [HBM],
        out_specs=[VMEM] * len(outs),
        out_shape=outs,
        scratch_shapes=[pltpu.SemaphoreType.DMA((PIECES,))],
        compiler_params=pltpu.CompilerParams(vmem_limit_bytes=46 << 20),
        cost_estimate=pl.CostEstimate(
            flops=2 * count * weight.size, bytes_accessed=2 * weight.size, transcendentals=0
        ),
    )(*args)
    return rest[0] if rest else feats, held, keep, send


def ahead_kernel(feats_ref, *refs):
    weights, (keep_ref, send_ref) = refs[:-2], refs[-2:]
    depth = sum(ref.shape[0] for ref in weights)
    at = 0
    for ref in weights:
        add_product(feats_ref, (at, depth), ref[...], keep_ref, send_ref)
        at += ref.shape[0]


def ahead(feats, *weights):
    half = jax.ShapeDtypeStruct((feats.shape[0] // 2, weights[0].shape[1]), F32)
    return pl.pallas_call(
        ahead_kernel,
        in_specs=[VMEM] * (1 + len(weights)),
        out_specs=[VMEM] * 2,
        out_shape=[half, half],
        compiler_params=pltpu.CompilerParams(vmem_limit_bytes=10 << 20),
        cost_estimate=pl.CostEstimate(
            flops=2 * feats.shape[0] * sum(w.size for w in weights), bytes_accessed=1 << 20, transcendentals=0
        ),
    )(feats, *weights)


def back_kernel(*refs, parts):
    grad_ref, weights, out_ref = refs[0], refs[1 : 1 + parts], refs[-1]
    at = 0
    for ref in weights:
        out = lax.dot_general(grad_ref[...], ref[...], COLS, preferred_element_type=F32)
        here = slice(at, at + ref.shape[0])
        out_ref[:, here] = out if len(refs) == parts + 2 else refs[-2][:, here] + out
        at += ref.shape[0]


def back(grad, weights, start=None):
    depth = sum(w.shape[0] for w in weights)
    args = (grad, *weights) if start is None else (grad, *weights, start)
    return pl.pallas_call(
        functools.partial(back_kernel, parts=len(weights)),
        in_specs=[VMEM] * len(args),
        out_specs=VMEM,
        out_shape=jax.ShapeDtypeStruct((grad.shape[0], depth), F32),
        compiler_params=pltpu.CompilerParams(vmem_limit_bytes=10 << 20),
        cost_estimate=pl.CostEstimate(flops=2 * grad.size * depth, bytes_accessed=1 << 20, transcendentals=0),
    )(*args)


def outer_kernel(rows_ref, grad_ref, *rest, base, scale):
    out_ref, buf, sem = rest[-3:]
    total, width = buf.shape
    wide = min(512, width)
    tall = min(512, total)
    sizes = [tall // 2] * 2 + [tall] * (total // tall - 1)
    copies = []
    top = 0
    for i, size in enumerate(sizes):
        for at in range(0, width, wide):
            acc = lax.dot_general(
                rows_ref[:, base + top : base + top + size],
                grad_ref[:, at : at + wide],
                DOWN,
                preferred_element_type=F32,
            )
            buf[top : top + size, at : at + wide] = (acc * scale).astype(BF16)
        source, target = buf.at[pl.ds(top, size), :], out_ref.at[pl.ds(base + top, size), :]
        copies.append(pltpu.make_async_copy(source, target, sem.at[i]))
        copies[-1].start()
        top += size
    for copy in copies:
        copy.wait()


def outer(rows, grad, scale, begin, share, whole=None):
    count, d_model = rows.shape
    width = grad.shape[1]
    part = d_model // share
    kernel = functools.partial(outer_kernel, base=begin * part, scale=scale)
    args = (rows, grad) if whole is None else (rows, grad, whole)
    return pl.pallas_call(
        kernel,
        in_specs=[VMEM, VMEM] + [HBM] * (len(args) - 2),
        out_specs=HBM,
        out_shape=jax.ShapeDtypeStruct((d_model, width), BF16),
        input_output_aliases={2: 0} if whole is not None else {},
        scratch_shapes=[pltpu.VMEM((part, width), BF16), pltpu.SemaphoreType.DMA((part // min(512, part) + 1,))],
        compiler_params=pltpu.CompilerParams(vmem_limit_bytes=32 << 20),
        cost_estimate=pl.CostEstimate(
            flops=2 * count * part * width,
            bytes_accessed=2 * part * width + 2 * count * (d_model + width),
            transcendentals=0,
        ),
    )(*args)


def shards(tokens, gate_weight, up_weight, cotangent):
    n_tp, n_dp = lax.axis_size("tp"), lax.axis_size("dp")
    assert n_dp == 4
    r = lax.axis_index("dp")
    _, rt, d_model = tokens.shape
    depth, _ = gate_weight.shape
    rows = rt * n_tp

    part = hold(tokens)
    for i, bit in enumerate(bits_of(n_tp)):
        near = swap(part if i else tokens, bit, 1)
        part = jnp.stack([part, near], axis=1).reshape(-1, rt, d_model)
    part = jnp.stack([part, swap(part, 0, 3)])
    far = swap(part, 0, 1)
    feats, gate_held, gate_keep, gate_send = gather_ahead(part, far, gate_weight)
    up_first = load(up_weight, 0, 2)
    up_second = load(up_weight, 1, 2)
    up_keep, up_send = ahead(feats, up_first, up_second)

    def partial(keep, send):
        other = swap(send, 0, 1)
        return (keep + other).astype(BF16)

    def summed(half):
        other = swap(half, 0, 3)
        other = jnp.concatenate([other[rows:], other[:rows]])
        return half.astype(F32) + other.astype(F32)

    half_gate = partial(gate_keep, gate_send)
    half_up = partial(up_keep, up_send)
    gate_pre = summed(half_gate)
    up_pre = summed(half_up)

    cot = reorder(cotangent[0], rt)
    far = swap(cot, 0, 3)
    cot = jnp.concatenate([cot, far])

    grad_hidden = cot.astype(F32)
    act, slope = swish_parts(gate_pre)
    d_up = (grad_hidden * act).astype(BF16)
    d_up, act, slope = lax.optimization_barrier((d_up, act, slope))
    far = swap(d_up, 0, 1)
    d_up = jnp.concatenate([d_up, far])
    total = back(d_up, (up_first, up_second))
    hidden = (act * up_pre)[:rows].astype(BF16)
    hidden = reorder(hidden, rt)[None]
    d_gate = (grad_hidden * up_pre * slope).astype(BF16)
    far = swap(d_gate, 0, 1)
    d_gate = jnp.concatenate([d_gate, far])
    total = back(d_gate, (gate_held,), total)

    total = total.reshape(2, 2, n_tp, rt, depth)
    for bit in reversed(bits_of(n_tp)):
        total = total.reshape(2, 2, -1, 2, rt, depth)
        total = total[:, :, :, 0] + swap(total[:, :, :, 1], bit, 0)
    total = total[:, :, 0]
    total = jnp.stack([total[:, 0], swap(total[:, 1], 0, 3)], axis=1)
    total = jnp.stack([total[0], swap(total[1], 0, 1)])
    total = [total[0, 0], total[1, 0], total[1, 1], total[0, 1]]
    for bit in (1, 2):
        total = [jnp.where(r & bit != 0, total[m ^ bit], total[m]) for m in range(n_dp)]
    grad_tokens = jnp.concatenate([v.astype(BF16) for v in total], axis=1)[None]

    inverse = 1.0 / n_dp
    grad_up = outer(feats, d_up, inverse, 0, 2)
    grad_up = outer(feats, d_up, inverse, 1, 2, grad_up)
    grad_gate = outer(feats, d_gate, inverse, 0, 2)
    grad_gate = outer(feats, d_gate, inverse, 1, 2, grad_gate)
    return hidden, grad_tokens, grad_gate, grad_up


def solution(mesh):
    in_specs = (P("dp", "tp", None), P("dp", "tp"), P("dp", "tp"), P("dp", None, "tp"))
    out_specs = (P("dp", None, "tp"), P("dp", "tp", None), P(None, "tp"), P(None, "tp"))

    return jax.shard_map(shards, mesh=mesh, in_specs=in_specs, out_specs=out_specs, check_vma=False)
```

```python
import functools

import jax
import jax.numpy as jnp
from jax import lax
from jax.experimental import pallas as pl
from jax.experimental.pallas import tpu as pltpu
from jax.sharding import PartitionSpec as P


F32 = jnp.float32
BF16 = jnp.bfloat16
VMEM = pl.BlockSpec(memory_space=pltpu.VMEM)
HBM = pl.BlockSpec(memory_space=pltpu.HBM)
COLS = (((1,), (1,)), ((), ()))
DOWN = (((0,), (0,)), ((), ()))
PIECES = 4


def swap(value, tp_mask, dp_mask):
    n_tp, n_dp = lax.axis_size("tp"), lax.axis_size("dp")
    pairs = [(t * n_dp + r, (t ^ tp_mask) * n_dp + (r ^ dp_mask)) for t in range(n_tp) for r in range(n_dp)]
    return lax.ppermute(value, ("tp", "dp"), pairs)


def bits_of(size):
    assert size & (size - 1) == 0
    return [1 << k for k in reversed(range(size.bit_length() - 1))]


def odd(value):
    return value.bit_count() % 2


def swish_parts(gate_pre):
    s = jax.nn.sigmoid(gate_pre)
    return gate_pre * s, s * (1.0 + gate_pre * (1.0 - s))


def hold_kernel(in_ref, out_ref):
    out_ref[...] = in_ref[...]


def hold(value):
    return pl.pallas_call(
        hold_kernel,
        in_specs=[VMEM],
        out_specs=VMEM,
        out_shape=jax.ShapeDtypeStruct(value.shape, value.dtype),
        compiler_params=pltpu.CompilerParams(vmem_limit_bytes=1 << 20),
        cost_estimate=pl.CostEstimate(flops=0, bytes_accessed=value.size, transcendentals=0),
    )(value)


def reorder_kernel(in_ref, out_ref, *, rt):
    rows = in_ref.shape[0]
    to = lax.broadcasted_iota(jnp.int32, (rows, rows), 0)
    source = lax.broadcasted_iota(jnp.int32, (rows, rows), 1)
    pick = ((to ^ (lax.axis_index("tp") * rt)) == source).astype(F32).astype(BF16)
    out_ref[...] = jnp.dot(pick, in_ref[...], preferred_element_type=F32).astype(BF16)


def reorder(value, rt):
    assert rt & (rt - 1) == 0
    return pl.pallas_call(
        functools.partial(reorder_kernel, rt=rt),
        in_specs=[VMEM],
        out_specs=VMEM,
        out_shape=jax.ShapeDtypeStruct(value.shape, BF16),
        compiler_params=pltpu.CompilerParams(vmem_limit_bytes=8 << 20),
        cost_estimate=pl.CostEstimate(flops=0, bytes_accessed=4 * value.size, transcendentals=0),
    )(value)


def load_kernel(weight_ref, out_ref, sem, *, begin):
    tall = out_ref.shape[0] // 2
    copies = [
        pltpu.make_async_copy(
            weight_ref.at[pl.ds(begin + i * tall, tall), :], out_ref.at[pl.ds(i * tall, tall), :], sem.at[i]
        )
        for i in range(2)
    ]
    for copy in copies:
        copy.start()
    for copy in copies:
        copy.wait()


def load(weight, part, parts):
    depth, width = weight.shape
    depth //= parts
    return pl.pallas_call(
        functools.partial(load_kernel, begin=part * depth),
        in_specs=[HBM],
        out_specs=VMEM,
        out_shape=jax.ShapeDtypeStruct((depth, width), BF16),
        scratch_shapes=[pltpu.SemaphoreType.DMA((2,))],
        compiler_params=pltpu.CompilerParams(vmem_limit_bytes=48 << 20),
        cost_estimate=pl.CostEstimate(flops=0, bytes_accessed=2 * depth * width, transcendentals=0),
    )(weight)


def add_product(feats_ref, at, weight, keep_ref, send_ref):
    half = keep_ref.shape[0]
    start = pl.multiple_of(lax.axis_index("dp") * at[1] + at[0], weight.shape[0])
    out = jnp.dot(feats_ref[:, pl.ds(start, weight.shape[0])], weight, preferred_element_type=F32)
    if at[0]:
        keep_ref[...] += out[:half]
        send_ref[...] += out[half:]
    else:
        keep_ref[...] = out[:half]
        send_ref[...] = out[half:]


def stream_product(feats_ref, copies, held_ref, keep_ref, send_ref):
    depth = held_ref.shape[0]
    tall = depth // PIECES
    for i, copy in enumerate(copies):
        copy.wait()
        add_product(feats_ref, (i * tall, depth), held_ref[i * tall : (i + 1) * tall, :], keep_ref, send_ref)


def start_copies(weight_ref, held_ref, sem):
    tall = held_ref.shape[0] // PIECES
    parts = [pl.ds(i * tall, tall) for i in range(PIECES)]
    copies = [
        pltpu.make_async_copy(weight_ref.at[at, :], held_ref.at[at, :], sem.at[i]) for i, at in enumerate(parts)
    ]
    for copy in copies:
        copy.start()
    return copies


def gather_kernel(part_ref, far_ref, weight_ref, held_ref, keep_ref, send_ref, feats_ref, sem):
    copies = start_copies(weight_ref, held_ref, sem)
    _, n_tp, rt, _ = part_ref.shape
    for core in range(2):
        for x in range(2):
            for k in range(n_tp):
                source = part_ref if odd(k) == core else far_ref
                row = ((core * 2 + x) * n_tp + k) * rt
                feats_ref[row : row + rt, :] = source[x, k]
    stream_product(feats_ref, copies, held_ref, keep_ref, send_ref)


def stream_kernel(feats_ref, weight_ref, held_ref, keep_ref, send_ref, sem):
    copies = start_copies(weight_ref, held_ref, sem)
    stream_product(feats_ref, copies, held_ref, keep_ref, send_ref)


def gather_ahead(part, far, weight):
    _, n_tp, rt, d_model = part.shape
    count, width = 4 * n_tp * rt, weight.shape[1]
    half = jax.ShapeDtypeStruct((count // 2, width), F32)
    outs = [jax.ShapeDtypeStruct(weight.shape, BF16), half, half]
    if n_tp <= 16:
        outs.append(jax.ShapeDtypeStruct((count, d_model), BF16))
        kernel, args = gather_kernel, (part, far, weight)
    else:
        mask = jnp.array([odd(k) == 1 for k in range(n_tp)])[None, :, None, None]
        feats = jnp.stack([jnp.where(mask, far, part), jnp.where(mask, part, far)]).reshape(count, d_model)
        kernel, args = stream_kernel, (feats, weight)
    held, keep, send, *rest = pl.pallas_call(
        kernel,
        in_specs=[VMEM] * (len(args) - 1) + [HBM],
        out_specs=[VMEM] * len(outs),
        out_shape=outs,
        scratch_shapes=[pltpu.SemaphoreType.DMA((PIECES,))],
        compiler_params=pltpu.CompilerParams(vmem_limit_bytes=46 << 20),
        cost_estimate=pl.CostEstimate(
            flops=2 * count * weight.size, bytes_accessed=2 * weight.size, transcendentals=0
        ),
    )(*args)
    return rest[0] if rest else feats, held, keep, send


def ahead_kernel(feats_ref, *refs):
    weights, (keep_ref, send_ref) = refs[:-2], refs[-2:]
    depth = sum(ref.shape[0] for ref in weights)
    at = 0
    for ref in weights:
        add_product(feats_ref, (at, depth), ref[...], keep_ref, send_ref)
        at += ref.shape[0]


def ahead(feats, *weights):
    half = jax.ShapeDtypeStruct((feats.shape[0] // 2, weights[0].shape[1]), F32)
    return pl.pallas_call(
        ahead_kernel,
        in_specs=[VMEM] * (1 + len(weights)),
        out_specs=[VMEM] * 2,
        out_shape=[half, half],
        compiler_params=pltpu.CompilerParams(vmem_limit_bytes=10 << 20),
        cost_estimate=pl.CostEstimate(
            flops=2 * feats.shape[0] * sum(w.size for w in weights), bytes_accessed=1 << 20, transcendentals=0
        ),
    )(feats, *weights)


def back_kernel(*refs, parts):
    grad_ref, weights, out_ref = refs[0], refs[1 : 1 + parts], refs[-1]
    at = 0
    for ref in weights:
        out = lax.dot_general(grad_ref[...], ref[...], COLS, preferred_element_type=F32)
        here = slice(at, at + ref.shape[0])
        out_ref[:, here] = out if len(refs) == parts + 2 else refs[-2][:, here] + out
        at += ref.shape[0]


def back(grad, weights, start=None):
    depth = sum(w.shape[0] for w in weights)
    args = (grad, *weights) if start is None else (grad, *weights, start)
    return pl.pallas_call(
        functools.partial(back_kernel, parts=len(weights)),
        in_specs=[VMEM] * len(args),
        out_specs=VMEM,
        out_shape=jax.ShapeDtypeStruct((grad.shape[0], depth), F32),
        compiler_params=pltpu.CompilerParams(vmem_limit_bytes=10 << 20),
        cost_estimate=pl.CostEstimate(flops=2 * grad.size * depth, bytes_accessed=1 << 20, transcendentals=0),
    )(*args)


def outer_kernel(rows_ref, grad_ref, *rest, base, scale):
    out_ref, buf, sem = rest[-3:]
    total, width = buf.shape
    wide = min(512, width)
    tall = min(512, total)
    sizes = [tall // 2] * 2 + [tall] * (total // tall - 1)
    copies = []
    top = 0
    for i, size in enumerate(sizes):
        for at in range(0, width, wide):
            acc = lax.dot_general(
                rows_ref[:, base + top : base + top + size],
                grad_ref[:, at : at + wide],
                DOWN,
                preferred_element_type=F32,
            )
            buf[top : top + size, at : at + wide] = (acc * scale).astype(BF16)
        source, target = buf.at[pl.ds(top, size), :], out_ref.at[pl.ds(base + top, size), :]
        copies.append(pltpu.make_async_copy(source, target, sem.at[i]))
        copies[-1].start()
        top += size
    for copy in copies:
        copy.wait()


def outer(rows, grad, scale, begin, share, whole=None):
    count, d_model = rows.shape
    width = grad.shape[1]
    part = d_model // share
    kernel = functools.partial(outer_kernel, base=begin * part, scale=scale)
    args = (rows, grad) if whole is None else (rows, grad, whole)
    return pl.pallas_call(
        kernel,
        in_specs=[VMEM, VMEM] + [HBM] * (len(args) - 2),
        out_specs=HBM,
        out_shape=jax.ShapeDtypeStruct((d_model, width), BF16),
        input_output_aliases={2: 0} if whole is not None else {},
        scratch_shapes=[pltpu.VMEM((part, width), BF16), pltpu.SemaphoreType.DMA((part // min(512, part) + 1,))],
        compiler_params=pltpu.CompilerParams(vmem_limit_bytes=32 << 20),
        cost_estimate=pl.CostEstimate(
            flops=2 * count * part * width,
            bytes_accessed=2 * part * width + 2 * count * (d_model + width),
            transcendentals=0,
        ),
    )(*args)


def shards(tokens, gate_weight, up_weight, cotangent):
    n_tp, n_dp = lax.axis_size("tp"), lax.axis_size("dp")
    assert n_dp == 4
    r = lax.axis_index("dp")
    _, rt, d_model = tokens.shape
    depth, _ = gate_weight.shape
    rows = rt * n_tp

    part = hold(tokens)
    for i, bit in enumerate(bits_of(n_tp)):
        near = swap(part if i else tokens, bit, 1)
        part = jnp.stack([part, near], axis=1).reshape(-1, rt, d_model)
    part = jnp.stack([part, swap(part, 0, 3)])
    far = swap(part, 0, 1)
    feats, gate_held, gate_keep, gate_send = gather_ahead(part, far, gate_weight)
    up_first = load(up_weight, 0, 2)
    up_second = load(up_weight, 1, 2)
    up_keep, up_send = ahead(feats, up_first, up_second)

    def partial(keep, send):
        other = swap(send, 0, 1)
        return (keep + other).astype(BF16)

    def summed(half):
        other = swap(half, 0, 3)
        other = jnp.concatenate([other[rows:], other[:rows]])
        return half.astype(F32) + other.astype(F32)

    half_gate = partial(gate_keep, gate_send)
    half_up = partial(up_keep, up_send)
    gate_pre = summed(half_gate)
    up_pre = summed(half_up)

    cot = reorder(cotangent[0], rt)
    far = swap(cot, 0, 3)
    cot = jnp.concatenate([cot, far])

    grad_hidden = cot.astype(F32)
    act, slope = swish_parts(gate_pre)
    d_up = (grad_hidden * act).astype(BF16)
    d_up, act, slope = lax.optimization_barrier((d_up, act, slope))
    far = swap(d_up, 0, 1)
    d_up = jnp.concatenate([d_up, far])
    total = back(d_up, (up_first, up_second))
    hidden = (act * up_pre)[:rows].astype(BF16)
    hidden = reorder(hidden, rt)[None]
    d_gate = (grad_hidden * up_pre * slope).astype(BF16)
    far = swap(d_gate, 0, 1)
    d_gate = jnp.concatenate([d_gate, far])
    total = back(d_gate, (gate_held,), total)

    total = total.reshape(2, 2, n_tp, rt, depth)
    for bit in reversed(bits_of(n_tp)):
        total = total.reshape(2, 2, -1, 2, rt, depth)
        total = total[:, :, :, 0] + swap(total[:, :, :, 1], bit, 0)
    total = total[:, :, 0]
    third = swap(total[0, 1], 0, 3)
    second = swap(total[1, 1], 0, 2)
    first = swap(total[1, 0], 0, 1)
    total = [total[0, 0], first, second, third]
    for bit in (1, 2):
        total = [jnp.where(r & bit != 0, total[m ^ bit], total[m]) for m in range(n_dp)]
    grad_tokens = jnp.concatenate([v.astype(BF16) for v in total], axis=1)[None]

    inverse = 1.0 / n_dp
    grad_up = outer(feats, d_up, inverse, 0, 2)
    grad_up = outer(feats, d_up, inverse, 1, 2, grad_up)
    grad_gate = outer(feats, d_gate, inverse, 0, 2)
    grad_gate = outer(feats, d_gate, inverse, 1, 2, grad_gate)
    return hidden, grad_tokens, grad_gate, grad_up


def solution(mesh):
    in_specs = (P("dp", "tp", None), P("dp", "tp"), P("dp", "tp"), P("dp", None, "tp"))
    out_specs = (P("dp", None, "tp"), P("dp", "tp", None), P(None, "tp"), P(None, "tp"))

    return jax.shard_map(shards, mesh=mesh, in_specs=in_specs, out_specs=out_specs, check_vma=False)
```

```python
import functools

import jax
import jax.numpy as jnp
from jax import lax
from jax.experimental import pallas as pl
from jax.experimental.pallas import tpu as pltpu
from jax.sharding import PartitionSpec as P


F32 = jnp.float32
BF16 = jnp.bfloat16
VMEM = pl.BlockSpec(memory_space=pltpu.VMEM)
HBM = pl.BlockSpec(memory_space=pltpu.HBM)
COLS = (((1,), (1,)), ((), ()))
DOWN = (((0,), (0,)), ((), ()))
PIECES = 4


def swap(value, tp_mask, dp_mask):
    n_tp, n_dp = lax.axis_size("tp"), lax.axis_size("dp")
    pairs = [(t * n_dp + r, (t ^ tp_mask) * n_dp + (r ^ dp_mask)) for t in range(n_tp) for r in range(n_dp)]
    return lax.ppermute(value, ("tp", "dp"), pairs)


def bits_of(size):
    assert size & (size - 1) == 0
    return [1 << k for k in reversed(range(size.bit_length() - 1))]


def odd(value):
    return value.bit_count() % 2


def swish_parts(gate_pre):
    s = jax.nn.sigmoid(gate_pre)
    return gate_pre * s, s * (1.0 + gate_pre * (1.0 - s))


def hold_kernel(in_ref, out_ref):
    out_ref[...] = in_ref[...]


def hold(value):
    return pl.pallas_call(
        hold_kernel,
        in_specs=[VMEM],
        out_specs=VMEM,
        out_shape=jax.ShapeDtypeStruct(value.shape, value.dtype),
        compiler_params=pltpu.CompilerParams(vmem_limit_bytes=1 << 20),
        cost_estimate=pl.CostEstimate(flops=0, bytes_accessed=value.size, transcendentals=0),
    )(value)


def reorder_kernel(in_ref, out_ref, *, rt):
    rows = in_ref.shape[0]
    to = lax.broadcasted_iota(jnp.int32, (rows, rows), 0)
    source = lax.broadcasted_iota(jnp.int32, (rows, rows), 1)
    pick = ((to ^ (lax.axis_index("tp") * rt)) == source).astype(F32).astype(BF16)
    out_ref[...] = jnp.dot(pick, in_ref[...], preferred_element_type=F32).astype(BF16)


def reorder(value, rt):
    assert rt & (rt - 1) == 0
    return pl.pallas_call(
        functools.partial(reorder_kernel, rt=rt),
        in_specs=[VMEM],
        out_specs=VMEM,
        out_shape=jax.ShapeDtypeStruct(value.shape, BF16),
        compiler_params=pltpu.CompilerParams(vmem_limit_bytes=8 << 20),
        cost_estimate=pl.CostEstimate(flops=0, bytes_accessed=4 * value.size, transcendentals=0),
    )(value)


def load_kernel(weight_ref, out_ref, sem, *, begin):
    tall = out_ref.shape[0] // 2
    copies = [
        pltpu.make_async_copy(
            weight_ref.at[pl.ds(begin + i * tall, tall), :], out_ref.at[pl.ds(i * tall, tall), :], sem.at[i]
        )
        for i in range(2)
    ]
    for copy in copies:
        copy.start()
    for copy in copies:
        copy.wait()


def load(weight, part, parts):
    depth, width = weight.shape
    depth //= parts
    return pl.pallas_call(
        functools.partial(load_kernel, begin=part * depth),
        in_specs=[HBM],
        out_specs=VMEM,
        out_shape=jax.ShapeDtypeStruct((depth, width), BF16),
        scratch_shapes=[pltpu.SemaphoreType.DMA((2,))],
        compiler_params=pltpu.CompilerParams(vmem_limit_bytes=48 << 20),
        cost_estimate=pl.CostEstimate(flops=0, bytes_accessed=2 * depth * width, transcendentals=0),
    )(weight)


def add_product(feats_ref, at, weight, keep_ref, send_ref):
    half = keep_ref.shape[0]
    start = pl.multiple_of(lax.axis_index("dp") * at[1] + at[0], weight.shape[0])
    out = jnp.dot(feats_ref[:, pl.ds(start, weight.shape[0])], weight, preferred_element_type=F32)
    if at[0]:
        keep_ref[...] += out[:half]
        send_ref[...] += out[half:]
    else:
        keep_ref[...] = out[:half]
        send_ref[...] = out[half:]


def stream_product(feats_ref, copies, held_ref, keep_ref, send_ref):
    depth = held_ref.shape[0]
    tall = depth // PIECES
    for i, copy in enumerate(copies):
        copy.wait()
        add_product(feats_ref, (i * tall, depth), held_ref[i * tall : (i + 1) * tall, :], keep_ref, send_ref)


def start_copies(weight_ref, held_ref, sem):
    tall = held_ref.shape[0] // PIECES
    parts = [pl.ds(i * tall, tall) for i in range(PIECES)]
    copies = [
        pltpu.make_async_copy(weight_ref.at[at, :], held_ref.at[at, :], sem.at[i]) for i, at in enumerate(parts)
    ]
    for copy in copies:
        copy.start()
    return copies


def gather_kernel(part_ref, far_ref, weight_ref, held_ref, keep_ref, send_ref, feats_ref, sem):
    copies = start_copies(weight_ref, held_ref, sem)
    _, n_tp, rt, _ = part_ref.shape
    for core in range(2):
        for x in range(2):
            for k in range(n_tp):
                source = part_ref if odd(k) == core else far_ref
                row = ((core * 2 + x) * n_tp + k) * rt
                feats_ref[row : row + rt, :] = source[x, k]
    stream_product(feats_ref, copies, held_ref, keep_ref, send_ref)


def stream_kernel(feats_ref, weight_ref, held_ref, keep_ref, send_ref, sem):
    copies = start_copies(weight_ref, held_ref, sem)
    stream_product(feats_ref, copies, held_ref, keep_ref, send_ref)


def gather_ahead(part, far, weight):
    _, n_tp, rt, d_model = part.shape
    count, width = 4 * n_tp * rt, weight.shape[1]
    half = jax.ShapeDtypeStruct((count // 2, width), F32)
    outs = [jax.ShapeDtypeStruct(weight.shape, BF16), half, half]
    if n_tp <= 16:
        outs.append(jax.ShapeDtypeStruct((count, d_model), BF16))
        kernel, args = gather_kernel, (part, far, weight)
    else:
        mask = jnp.array([odd(k) == 1 for k in range(n_tp)])[None, :, None, None]
        feats = jnp.stack([jnp.where(mask, far, part), jnp.where(mask, part, far)]).reshape(count, d_model)
        kernel, args = stream_kernel, (feats, weight)
    held, keep, send, *rest = pl.pallas_call(
        kernel,
        in_specs=[VMEM] * (len(args) - 1) + [HBM],
        out_specs=[VMEM] * len(outs),
        out_shape=outs,
        scratch_shapes=[pltpu.SemaphoreType.DMA((PIECES,))],
        compiler_params=pltpu.CompilerParams(vmem_limit_bytes=46 << 20),
        cost_estimate=pl.CostEstimate(
            flops=2 * count * weight.size, bytes_accessed=2 * weight.size, transcendentals=0
        ),
    )(*args)
    return rest[0] if rest else feats, held, keep, send


def ahead_kernel(feats_ref, *refs):
    weights, (keep_ref, send_ref) = refs[:-2], refs[-2:]
    depth = sum(ref.shape[0] for ref in weights)
    at = 0
    for ref in weights:
        add_product(feats_ref, (at, depth), ref[...], keep_ref, send_ref)
        at += ref.shape[0]


def ahead(feats, *weights):
    half = jax.ShapeDtypeStruct((feats.shape[0] // 2, weights[0].shape[1]), F32)
    return pl.pallas_call(
        ahead_kernel,
        in_specs=[VMEM] * (1 + len(weights)),
        out_specs=[VMEM] * 2,
        out_shape=[half, half],
        compiler_params=pltpu.CompilerParams(vmem_limit_bytes=10 << 20),
        cost_estimate=pl.CostEstimate(
            flops=2 * feats.shape[0] * sum(w.size for w in weights), bytes_accessed=1 << 20, transcendentals=0
        ),
    )(feats, *weights)


def back_kernel(*refs, parts):
    grad_ref, weights, out_ref = refs[0], refs[1 : 1 + parts], refs[-1]
    at = 0
    for ref in weights:
        out = lax.dot_general(grad_ref[...], ref[...], COLS, preferred_element_type=F32)
        here = slice(at, at + ref.shape[0])
        out_ref[:, here] = out if len(refs) == parts + 2 else refs[-2][:, here] + out
        at += ref.shape[0]


def back(grad, weights, start=None):
    depth = sum(w.shape[0] for w in weights)
    args = (grad, *weights) if start is None else (grad, *weights, start)
    return pl.pallas_call(
        functools.partial(back_kernel, parts=len(weights)),
        in_specs=[VMEM] * len(args),
        out_specs=VMEM,
        out_shape=jax.ShapeDtypeStruct((grad.shape[0], depth), F32),
        compiler_params=pltpu.CompilerParams(vmem_limit_bytes=10 << 20),
        cost_estimate=pl.CostEstimate(flops=2 * grad.size * depth, bytes_accessed=1 << 20, transcendentals=0),
    )(*args)


def outer_kernel(rows_ref, grad_ref, *rest, base, scale):
    out_ref, buf, sem = rest[-3:]
    total, width = buf.shape
    wide = min(512, width)
    tall = min(512, total)
    sizes = [tall // 2] * 2 + [tall] * (total // tall - 1)
    copies = []
    top = 0
    for i, size in enumerate(sizes):
        for at in range(0, width, wide):
            acc = lax.dot_general(
                rows_ref[:, base + top : base + top + size],
                grad_ref[:, at : at + wide],
                DOWN,
                preferred_element_type=F32,
            )
            buf[top : top + size, at : at + wide] = (acc * scale).astype(BF16)
        source, target = buf.at[pl.ds(top, size), :], out_ref.at[pl.ds(base + top, size), :]
        copies.append(pltpu.make_async_copy(source, target, sem.at[i]))
        copies[-1].start()
        top += size
    for copy in copies:
        copy.wait()


def outer(rows, grad, scale, begin, share, whole=None):
    count, d_model = rows.shape
    width = grad.shape[1]
    part = d_model // share
    kernel = functools.partial(outer_kernel, base=begin * part, scale=scale)
    args = (rows, grad) if whole is None else (rows, grad, whole)
    return pl.pallas_call(
        kernel,
        in_specs=[VMEM, VMEM] + [HBM] * (len(args) - 2),
        out_specs=HBM,
        out_shape=jax.ShapeDtypeStruct((d_model, width), BF16),
        input_output_aliases={2: 0} if whole is not None else {},
        scratch_shapes=[pltpu.VMEM((part, width), BF16), pltpu.SemaphoreType.DMA((part // min(512, part) + 1,))],
        compiler_params=pltpu.CompilerParams(vmem_limit_bytes=32 << 20),
        cost_estimate=pl.CostEstimate(
            flops=2 * count * part * width,
            bytes_accessed=2 * part * width + 2 * count * (d_model + width),
            transcendentals=0,
        ),
    )(*args)


def shards(tokens, gate_weight, up_weight, cotangent):
    n_tp, n_dp = lax.axis_size("tp"), lax.axis_size("dp")
    assert n_dp == 4
    r = lax.axis_index("dp")
    _, rt, d_model = tokens.shape
    depth, _ = gate_weight.shape
    rows = rt * n_tp

    part = hold(tokens)
    for i, bit in enumerate(bits_of(n_tp)):
        near = swap(part if i else tokens, bit, 1)
        part = jnp.stack([part, near], axis=1).reshape(-1, rt, d_model)
    part = jnp.stack([part, swap(part, 0, 3)])
    far = swap(part, 0, 1)
    feats, gate_held, gate_keep, gate_send = gather_ahead(part, far, gate_weight)
    up_first = load(up_weight, 0, 2)
    up_second = load(up_weight, 1, 2)
    up_keep, up_send = ahead(feats, up_first, up_second)

    def partial(keep, send):
        other = swap(send, 0, 1)
        return (keep + other).astype(BF16)

    def summed(half):
        other = swap(half, 0, 3)
        other = jnp.concatenate([other[rows:], other[:rows]])
        return half.astype(F32) + other.astype(F32)

    half_gate = partial(gate_keep, gate_send)
    half_up = partial(up_keep, up_send)
    gate_pre = summed(half_gate)
    up_pre = summed(half_up)

    cot = swap(cotangent[0], 0, 3)
    cot = reorder(jnp.concatenate([cotangent[0], cot]), rt)

    grad_hidden = cot.astype(F32)
    act, slope = swish_parts(gate_pre)
    d_up = (grad_hidden * act).astype(BF16)
    d_up, act, slope = lax.optimization_barrier((d_up, act, slope))
    far = swap(d_up, 0, 1)
    d_up = jnp.concatenate([d_up, far])
    total = back(d_up, (up_first, up_second))
    hidden = (act * up_pre)[:rows].astype(BF16)
    hidden = reorder(hidden, rt)[None]
    d_gate = (grad_hidden * up_pre * slope).astype(BF16)
    far = swap(d_gate, 0, 1)
    d_gate = jnp.concatenate([d_gate, far])
    total = back(d_gate, (gate_held,), total)

    total = total.reshape(2, 2, n_tp, rt, depth)
    for bit in reversed(bits_of(n_tp)):
        total = total.reshape(2, 2, -1, 2, rt, depth)
        total = total[:, :, :, 0] + swap(total[:, :, :, 1], bit, 0)
    total = total[:, :, 0]
    third = swap(total[0, 1], 0, 3)
    second = swap(total[1, 1], 0, 2)
    first = swap(total[1, 0], 0, 1)
    total = [total[0, 0], first, second, third]
    for bit in (1, 2):
        total = [jnp.where(r & bit != 0, total[m ^ bit], total[m]) for m in range(n_dp)]
    grad_tokens = jnp.concatenate([v.astype(BF16) for v in total], axis=1)[None]

    inverse = 1.0 / n_dp
    grad_up = outer(feats, d_up, inverse, 0, 2)
    grad_up = outer(feats, d_up, inverse, 1, 2, grad_up)
    grad_gate = outer(feats, d_gate, inverse, 0, 2)
    grad_gate = outer(feats, d_gate, inverse, 1, 2, grad_gate)
    return hidden, grad_tokens, grad_gate, grad_up


def solution(mesh):
    in_specs = (P("dp", "tp", None), P("dp", "tp"), P("dp", "tp"), P("dp", None, "tp"))
    out_specs = (P("dp", None, "tp"), P("dp", "tp", None), P(None, "tp"), P(None, "tp"))

    return jax.shard_map(shards, mesh=mesh, in_specs=in_specs, out_specs=out_specs, check_vma=False)
```

```python
import functools

import jax
import jax.numpy as jnp
from jax import lax
from jax.experimental import pallas as pl
from jax.experimental.pallas import tpu as pltpu
from jax.sharding import PartitionSpec as P


F32 = jnp.float32
BF16 = jnp.bfloat16
VMEM = pl.BlockSpec(memory_space=pltpu.VMEM)
HBM = pl.BlockSpec(memory_space=pltpu.HBM)
COLS = (((1,), (1,)), ((), ()))
DOWN = (((0,), (0,)), ((), ()))
PIECES = 8


def swap(value, tp_mask, dp_mask):
    n_tp, n_dp = lax.axis_size("tp"), lax.axis_size("dp")
    pairs = [(t * n_dp + r, (t ^ tp_mask) * n_dp + (r ^ dp_mask)) for t in range(n_tp) for r in range(n_dp)]
    return lax.ppermute(value, ("tp", "dp"), pairs)


def bits_of(size):
    assert size & (size - 1) == 0
    return [1 << k for k in reversed(range(size.bit_length() - 1))]


def odd(value):
    return value.bit_count() % 2


def swish_parts(gate_pre):
    s = jax.nn.sigmoid(gate_pre)
    return gate_pre * s, s * (1.0 + gate_pre * (1.0 - s))


def hold_kernel(in_ref, out_ref):
    out_ref[...] = in_ref[...]


def hold(value):
    return pl.pallas_call(
        hold_kernel,
        in_specs=[VMEM],
        out_specs=VMEM,
        out_shape=jax.ShapeDtypeStruct(value.shape, value.dtype),
        compiler_params=pltpu.CompilerParams(vmem_limit_bytes=1 << 20),
        cost_estimate=pl.CostEstimate(flops=0, bytes_accessed=value.size, transcendentals=0),
    )(value)


def reorder_kernel(in_ref, out_ref, *, rt):
    rows = in_ref.shape[0]
    to = lax.broadcasted_iota(jnp.int32, (rows, rows), 0)
    source = lax.broadcasted_iota(jnp.int32, (rows, rows), 1)
    pick = ((to ^ (lax.axis_index("tp") * rt)) == source).astype(F32).astype(BF16)
    out_ref[...] = jnp.dot(pick, in_ref[...], preferred_element_type=F32).astype(BF16)


def reorder(value, rt):
    assert rt & (rt - 1) == 0
    return pl.pallas_call(
        functools.partial(reorder_kernel, rt=rt),
        in_specs=[VMEM],
        out_specs=VMEM,
        out_shape=jax.ShapeDtypeStruct(value.shape, BF16),
        compiler_params=pltpu.CompilerParams(vmem_limit_bytes=8 << 20),
        cost_estimate=pl.CostEstimate(flops=0, bytes_accessed=4 * value.size, transcendentals=0),
    )(value)


def load_kernel(weight_ref, out_ref, sem, *, begin):
    tall = out_ref.shape[0] // 2
    copies = [
        pltpu.make_async_copy(
            weight_ref.at[pl.ds(begin + i * tall, tall), :], out_ref.at[pl.ds(i * tall, tall), :], sem.at[i]
        )
        for i in range(2)
    ]
    for copy in copies:
        copy.start()
    for copy in copies:
        copy.wait()


def load(weight, part, parts):
    depth, width = weight.shape
    depth //= parts
    return pl.pallas_call(
        functools.partial(load_kernel, begin=part * depth),
        in_specs=[HBM],
        out_specs=VMEM,
        out_shape=jax.ShapeDtypeStruct((depth, width), BF16),
        scratch_shapes=[pltpu.SemaphoreType.DMA((2,))],
        compiler_params=pltpu.CompilerParams(vmem_limit_bytes=48 << 20),
        cost_estimate=pl.CostEstimate(flops=0, bytes_accessed=2 * depth * width, transcendentals=0),
    )(weight)


def add_product(feats_ref, at, weight, keep_ref, send_ref):
    half = keep_ref.shape[0]
    start = pl.multiple_of(lax.axis_index("dp") * at[1] + at[0], weight.shape[0])
    out = jnp.dot(feats_ref[:, pl.ds(start, weight.shape[0])], weight, preferred_element_type=F32)
    if at[0]:
        keep_ref[...] += out[:half]
        send_ref[...] += out[half:]
    else:
        keep_ref[...] = out[:half]
        send_ref[...] = out[half:]


def stream_product(feats_ref, copies, held_ref, keep_ref, send_ref):
    depth = held_ref.shape[0]
    tall = depth // PIECES
    for i, copy in enumerate(copies):
        copy.wait()
        add_product(feats_ref, (i * tall, depth), held_ref[i * tall : (i + 1) * tall, :], keep_ref, send_ref)


def start_copies(weight_ref, held_ref, sem):
    tall = held_ref.shape[0] // PIECES
    parts = [pl.ds(i * tall, tall) for i in range(PIECES)]
    copies = [
        pltpu.make_async_copy(weight_ref.at[at, :], held_ref.at[at, :], sem.at[i]) for i, at in enumerate(parts)
    ]
    for copy in copies:
        copy.start()
    return copies


def gather_kernel(part_ref, far_ref, weight_ref, held_ref, keep_ref, send_ref, feats_ref, sem):
    copies = start_copies(weight_ref, held_ref, sem)
    _, n_tp, rt, _ = part_ref.shape
    for core in range(2):
        for x in range(2):
            for k in range(n_tp):
                source = part_ref if odd(k) == core else far_ref
                row = ((core * 2 + x) * n_tp + k) * rt
                feats_ref[row : row + rt, :] = source[x, k]
    stream_product(feats_ref, copies, held_ref, keep_ref, send_ref)


def stream_kernel(feats_ref, weight_ref, held_ref, keep_ref, send_ref, sem):
    copies = start_copies(weight_ref, held_ref, sem)
    stream_product(feats_ref, copies, held_ref, keep_ref, send_ref)


def gather_ahead(part, far, weight):
    _, n_tp, rt, d_model = part.shape
    count, width = 4 * n_tp * rt, weight.shape[1]
    half = jax.ShapeDtypeStruct((count // 2, width), F32)
    outs = [jax.ShapeDtypeStruct(weight.shape, BF16), half, half]
    if n_tp <= 16:
        outs.append(jax.ShapeDtypeStruct((count, d_model), BF16))
        kernel, args = gather_kernel, (part, far, weight)
    else:
        mask = jnp.array([odd(k) == 1 for k in range(n_tp)])[None, :, None, None]
        feats = jnp.stack([jnp.where(mask, far, part), jnp.where(mask, part, far)]).reshape(count, d_model)
        kernel, args = stream_kernel, (feats, weight)
    held, keep, send, *rest = pl.pallas_call(
        kernel,
        in_specs=[VMEM] * (len(args) - 1) + [HBM],
        out_specs=[VMEM] * len(outs),
        out_shape=outs,
        scratch_shapes=[pltpu.SemaphoreType.DMA((PIECES,))],
        compiler_params=pltpu.CompilerParams(vmem_limit_bytes=46 << 20),
        cost_estimate=pl.CostEstimate(
            flops=2 * count * weight.size, bytes_accessed=2 * weight.size, transcendentals=0
        ),
    )(*args)
    return rest[0] if rest else feats, held, keep, send


def ahead_kernel(feats_ref, *refs):
    weights, (keep_ref, send_ref) = refs[:-2], refs[-2:]
    depth = sum(ref.shape[0] for ref in weights)
    at = 0
    for ref in weights:
        add_product(feats_ref, (at, depth), ref[...], keep_ref, send_ref)
        at += ref.shape[0]


def ahead(feats, *weights):
    half = jax.ShapeDtypeStruct((feats.shape[0] // 2, weights[0].shape[1]), F32)
    return pl.pallas_call(
        ahead_kernel,
        in_specs=[VMEM] * (1 + len(weights)),
        out_specs=[VMEM] * 2,
        out_shape=[half, half],
        compiler_params=pltpu.CompilerParams(vmem_limit_bytes=10 << 20),
        cost_estimate=pl.CostEstimate(
            flops=2 * feats.shape[0] * sum(w.size for w in weights), bytes_accessed=1 << 20, transcendentals=0
        ),
    )(feats, *weights)


def back_kernel(*refs, parts):
    grad_ref, weights, out_ref = refs[0], refs[1 : 1 + parts], refs[-1]
    at = 0
    for ref in weights:
        out = lax.dot_general(grad_ref[...], ref[...], COLS, preferred_element_type=F32)
        here = slice(at, at + ref.shape[0])
        out_ref[:, here] = out if len(refs) == parts + 2 else refs[-2][:, here] + out
        at += ref.shape[0]


def back(grad, weights, start=None):
    depth = sum(w.shape[0] for w in weights)
    args = (grad, *weights) if start is None else (grad, *weights, start)
    return pl.pallas_call(
        functools.partial(back_kernel, parts=len(weights)),
        in_specs=[VMEM] * len(args),
        out_specs=VMEM,
        out_shape=jax.ShapeDtypeStruct((grad.shape[0], depth), F32),
        compiler_params=pltpu.CompilerParams(vmem_limit_bytes=10 << 20),
        cost_estimate=pl.CostEstimate(flops=2 * grad.size * depth, bytes_accessed=1 << 20, transcendentals=0),
    )(*args)


def outer_kernel(rows_ref, grad_ref, *rest, base, scale, carried, after, placed):
    rest = list(rest)
    after_ref = rest.pop(0) if after is not None else None
    carry_ref = rest.pop(0) if carried else None
    if placed:
        rest.pop(0)
    out_ref = rest.pop(0)
    next_ref = rest.pop(0) if after is not None else None
    buf, sem = rest
    total, width = buf.shape
    wide = min(512, width)
    tall = min(512, total)

    def block(source_ref, row, size, target_ref, top):
        for at in range(0, width, wide):
            acc = lax.dot_general(
                rows_ref[:, row : row + size], source_ref[:, at : at + wide], DOWN, preferred_element_type=F32
            )
            target_ref[top : top + size, at : at + wide] = (acc * scale).astype(BF16)

    copies = []
    top = 0
    for i, size in enumerate([tall // 2] * 2 + [tall] * (total // tall - 1)):
        if i == 0 and carried:
            source = carry_ref
        else:
            block(grad_ref, base + top, size, buf, top)
            source = buf.at[pl.ds(top, size), :]
        copies.append(pltpu.make_async_copy(source, out_ref.at[pl.ds(base + top, size), :], sem.at[i]))
        copies[-1].start()
        top += size
    if after is not None:
        block(after_ref, after, tall // 2, next_ref, 0)
    for copy in copies:
        copy.wait()


def outer(rows, grad, scale, begin, share, whole=None, carry=None, after=None):
    count, d_model = rows.shape
    width = grad.shape[1]
    part = d_model // share
    ahead_rows = min(512, part) // 2
    args, specs = [rows, grad], [VMEM, VMEM]
    outs, out_specs = [jax.ShapeDtypeStruct((d_model, width), BF16)], [HBM]
    if after is not None:
        args.append(after[0])
        outs.append(jax.ShapeDtypeStruct((ahead_rows, width), BF16))
        out_specs.append(VMEM)
    if carry is not None:
        args.append(carry)
    specs = [VMEM] * len(args)
    if whole is not None:
        args.append(whole)
        specs.append(HBM)
    kernel = functools.partial(
        outer_kernel,
        base=begin * part,
        scale=scale,
        carried=carry is not None,
        after=None if after is None else after[1] * part,
        placed=whole is not None,
    )
    return pl.pallas_call(
        kernel,
        in_specs=specs,
        out_specs=out_specs,
        out_shape=outs,
        input_output_aliases={len(args) - 1: 0} if whole is not None else {},
        scratch_shapes=[pltpu.VMEM((part, width), BF16), pltpu.SemaphoreType.DMA((part // min(512, part) + 1,))],
        compiler_params=pltpu.CompilerParams(vmem_limit_bytes=32 << 20),
        cost_estimate=pl.CostEstimate(
            flops=2 * count * part * width,
            bytes_accessed=2 * part * width + 2 * count * (d_model + width),
            transcendentals=0,
        ),
    )(*args)


def place_kernel(*refs):
    out_ref = refs[-1]
    depth = refs[0].shape[1]
    for j, ref in enumerate(refs[:-1]):
        at = pl.multiple_of((lax.axis_index("dp") ^ j) * depth, depth)
        out_ref[:, pl.ds(at, depth)] = ref[...].astype(BF16)


def place(blocks):
    rt, depth = blocks[0].shape
    return pl.pallas_call(
        place_kernel,
        in_specs=[VMEM] * len(blocks),
        out_specs=VMEM,
        out_shape=jax.ShapeDtypeStruct((rt, depth * len(blocks)), BF16),
        compiler_params=pltpu.CompilerParams(vmem_limit_bytes=4 << 20),
        cost_estimate=pl.CostEstimate(flops=0, bytes_accessed=8 * rt * depth * len(blocks), transcendentals=0),
    )(*blocks)


def shards(tokens, gate_weight, up_weight, cotangent):
    n_tp, n_dp = lax.axis_size("tp"), lax.axis_size("dp")
    assert n_dp == 4
    _, rt, d_model = tokens.shape
    depth, _ = gate_weight.shape
    rows = rt * n_tp

    part = hold(tokens)
    for i, bit in enumerate(bits_of(n_tp)):
        near = swap(part if i else tokens, bit, 1)
        part = jnp.stack([part, near], axis=1).reshape(-1, rt, d_model)
    part = jnp.stack([part, swap(part, 0, 3)])
    far = swap(part, 0, 1)
    feats, gate_held, gate_keep, gate_send = gather_ahead(part, far, gate_weight)
    up_first = load(up_weight, 0, 2)
    up_second = load(up_weight, 1, 2)
    up_keep, up_send = ahead(feats, up_first, up_second)

    def partial(keep, send):
        other = swap(send, 0, 1)
        return (keep + other).astype(BF16)

    def summed(half):
        other = swap(half, 0, 3)
        other = jnp.concatenate([other[rows:], other[:rows]])
        return half.astype(F32) + other.astype(F32)

    half_gate = partial(gate_keep, gate_send)
    half_up = partial(up_keep, up_send)
    gate_pre = summed(half_gate)
    up_pre = summed(half_up)

    cot = swap(cotangent[0], 0, 3)
    cot = reorder(jnp.concatenate([cotangent[0], cot]), rt)

    grad_hidden = cot.astype(F32)
    act, slope = swish_parts(gate_pre)
    d_up = (grad_hidden * act).astype(BF16)
    d_up, act, slope = lax.optimization_barrier((d_up, act, slope))
    far = swap(d_up, 0, 1)
    d_up = jnp.concatenate([d_up, far])
    total = back(d_up, (up_first, up_second))
    hidden = (act * up_pre)[:rows].astype(BF16)
    hidden = reorder(hidden, rt)[None]
    d_gate = (grad_hidden * up_pre * slope).astype(BF16)
    far = swap(d_gate, 0, 1)
    d_gate = jnp.concatenate([d_gate, far])
    total = back(d_gate, (gate_held,), total)

    total = total.reshape(2, 2, n_tp, rt, depth)
    for bit in reversed(bits_of(n_tp)):
        total = total.reshape(2, 2, -1, 2, rt, depth)
        total = total[:, :, :, 0] + swap(total[:, :, :, 1], bit, 0)
    total = total[:, :, 0]
    third = swap(total[0, 1], 0, 3)
    second = swap(total[1, 1], 0, 2)
    first = swap(total[1, 0], 0, 1)
    total = [total[0, 0], first, second, third]
    grad_tokens = place(total)[None]

    inverse = 1.0 / n_dp
    grad_up, carry = outer(feats, d_up, inverse, 0, 2, after=(d_up, 1))
    grad_up, carry = outer(feats, d_up, inverse, 1, 2, grad_up, carry, after=(d_gate, 0))
    grad_gate, carry = outer(feats, d_gate, inverse, 0, 2, None, carry, after=(d_gate, 1))
    (grad_gate,) = outer(feats, d_gate, inverse, 1, 2, grad_gate, carry)
    return hidden, grad_tokens, grad_gate, grad_up


def solution(mesh):
    in_specs = (P("dp", "tp", None), P("dp", "tp"), P("dp", "tp"), P("dp", None, "tp"))
    out_specs = (P("dp", None, "tp"), P("dp", "tp", None), P(None, "tp"), P(None, "tp"))

    return jax.shard_map(shards, mesh=mesh, in_specs=in_specs, out_specs=out_specs, check_vma=False)
```
